256 devices in a mesh: wide: 64 (over y, z, core), leaf: 4 (over x).
Axes of the slice: x: 4, y: 4, z: 8, core: 2. Of those that a mesh axis runs over, the one named last changes fastest.
Arguments:
- leaf_maps: float32 [64, 4, 2, 2, 512, 512], P('wide', 'leaf'), may hold values from -0.36 to 1.01
- angles: float32 [32], replicated, may hold values from -1.2 to 1.2
Outputs:
- reflected: float32 [64, 2, 64, 512], P('wide', None, 'leaf')
- transmitted: float32 [64, 2, 64, 512], P('wide', None, 'leaf')
The draws below stay inside these ranges and needn't reach their ends.
All inputs are finite; a program needn't handle non-finite values.
Results may differ from the reference program's by a relative error of at most 0.0003.
Values sent between devices are 32-bit elements; how exact they have to be, the bound alone decides.
A program may use at most 320 MiB of HBM per device.

```python
import math
import jax
import jax.numpy as jnp
from jax import lax

P_SIZE = 128
POLS = 2
ANG = 32
LEAVES = 4
NPT = 512
SUBS = 64


def draw_leaf_maps(key, part):
    shape_all = (SUBS, LEAVES, POLS, 2, NPT, NPT)
    base = jax.random.truncated_normal(key, -4.0, 4.0, shape_all, jnp.float32)
    row_ids = jnp.arange(NPT, dtype=jnp.int32)[:, None]
    col_ids = jnp.arange(NPT, dtype=jnp.int32)[None, :]
    row_edge = row_ids // P_SIZE
    col_edge = col_ids // P_SIZE
    table = jnp.array([[0.2, 0.15, 0.35, 0.35], [0.15, 0.2, 0.35, 0.35], [0.35, 0.35, 0.5, 0.2], [0.35, 0.35, 0.2, 0.5]], jnp.float32)
    block_scale = table[row_edge, col_edge] / math.sqrt(2.0 * P_SIZE)
    same_point = row_ids % P_SIZE == col_ids % P_SIZE
    across = jnp.logical_and(row_edge + col_edge == 1, row_edge != col_edge)
    upward = jnp.logical_and(row_edge + col_edge == 5, row_edge != col_edge)
    selfward = jnp.logical_and(row_edge == col_edge, row_edge >= 2)
    real_diag = jnp.where(jnp.logical_and(same_point, across), 0.9, 0.0) + jnp.where(jnp.logical_and(same_point, upward), 0.5, 0.0)
    imag_diag = jnp.where(jnp.logical_and(same_point, selfward), 0.5, 0.0)
    fixed_part = jnp.stack([real_diag, imag_diag]).astype(jnp.float32)
    return base * block_scale + fixed_part


def setup_inputs(seed: int = 0) -> dict:
    keys = jax.random.split(jax.random.key(seed), 3)
    return {
        "leaf_maps": draw_leaf_maps(jax.random.fold_in(keys[2], 71), 0),
        "angles": jnp.clip(jax.random.uniform(keys[1], (ANG,), jnp.float32, -1.2, 1.2), -1.2, 1.2),
    }


precise = lax.Precision.HIGHEST
wavenumber = 12.0

def plain_dot(left_mat, right_mat):
    return jnp.dot(left_mat.astype(jnp.float32), right_mat.astype(jnp.float32), precision=precise, preferred_element_type=jnp.float32)

def complex_dot(left_mat, right_mat):
    real_part = plain_dot(left_mat[0], right_mat[0]) - plain_dot(left_mat[1], right_mat[1])
    imag_part = plain_dot(left_mat[0], right_mat[1]) + plain_dot(left_mat[1], right_mat[0])
    return jnp.stack([real_part, imag_part])

def side_dot(vectors, matrix):
    return lax.dot_general(vectors.astype(jnp.float32), matrix.astype(jnp.float32), (((1,), (1,)), ((), ())), precision=precise, preferred_element_type=jnp.float32)

def complex_apply(matrix, vectors):
    real_part = side_dot(vectors[0], matrix[0]) - side_dot(vectors[1], matrix[1])
    imag_part = side_dot(vectors[0], matrix[1]) + side_dot(vectors[1], matrix[0])
    return jnp.stack([real_part, imag_part])

def complex_solve(system, right_mat):
    size_n = system.shape[1]
    upper_band = jnp.concatenate([system[0], -system[1]], 1)
    lower_band = jnp.concatenate([system[1], system[0]], 1)
    big_mat = jnp.concatenate([upper_band, lower_band], 0)
    stacked = jnp.concatenate([right_mat[0], right_mat[1]], 0)
    normal = lax.dot_general(big_mat.astype(jnp.float32), big_mat.astype(jnp.float32), (((0,), (0,)), ((), ())), precision=precise, preferred_element_type=jnp.float32)
    projected = lax.dot_general(big_mat.astype(jnp.float32), stacked.astype(jnp.float32), (((0,), (0,)), ((), ())), precision=precise, preferred_element_type=jnp.float32)
    factor = jnp.linalg.cholesky(normal)
    solution = jax.scipy.linalg.cho_solve((factor, True), projected)
    return jnp.stack([solution[:size_n], solution[size_n:]])

def block_take(matrix, row_list, col_list):
    row_cat = jnp.concatenate([matrix[:, start_at:stop_at] for start_at, stop_at in row_list], 1)
    return jnp.concatenate([row_cat[:, :, start_at:stop_at] for start_at, stop_at in col_list], 2)

def merge_setup(map_lower, map_upper, side_pts, edge_pts, keeping):
    total_pts = 2 * side_pts + 2 * edge_pts
    lower_ext = 2 * side_pts + (edge_pts if keeping else 0)
    lower_outer = [(0, lower_ext)]
    lower_inner = [(2 * side_pts + edge_pts, total_pts)]
    upper_outer = [(0, 2 * side_pts)] + ([(2 * side_pts + edge_pts, total_pts)] if keeping else [])
    upper_inner = [(2 * side_pts, 2 * side_pts + edge_pts)]
    alpha_outer = block_take(map_lower, lower_outer, lower_outer)
    alpha_reach = block_take(map_lower, lower_outer, lower_inner)
    alpha_inward = block_take(map_lower, lower_inner, lower_outer)
    alpha_inner = block_take(map_lower, lower_inner, lower_inner)
    beta_outer = block_take(map_upper, upper_outer, upper_outer)
    beta_reach = block_take(map_upper, upper_outer, upper_inner)
    beta_inward = block_take(map_upper, upper_inner, upper_outer)
    beta_inner = block_take(map_upper, upper_inner, upper_inner)
    identity_mat = jnp.stack([jnp.eye(edge_pts, dtype=jnp.float32), jnp.zeros((edge_pts, edge_pts), jnp.float32)])
    system = identity_mat - complex_dot(beta_inner, alpha_inner)
    right_mat = jnp.concatenate([-complex_dot(beta_inner, alpha_inward), beta_inward], 2)
    solved = complex_solve(system, right_mat)
    blocks = (alpha_outer, alpha_reach, alpha_inward, alpha_inner, beta_outer, beta_reach)
    return (blocks, solved)

def rows_lower(blocks, solved):
    alpha_outer, alpha_reach = (blocks[0], blocks[1])
    upper_count = solved.shape[2] - alpha_outer.shape[2]
    padded = jnp.concatenate([alpha_outer, jnp.zeros((2, alpha_outer.shape[1], upper_count), jnp.float32)], 2)
    return padded - complex_dot(alpha_reach, solved)

def rows_upper(blocks, solved):
    alpha_inward, alpha_inner, beta_outer, beta_reach = (blocks[2], blocks[3], blocks[4], blocks[5])
    leading = jnp.concatenate([-complex_dot(beta_reach, alpha_inward), beta_outer], 2)
    return leading + complex_dot(complex_dot(beta_reach, alpha_inner), solved)

def order_spans(side_pts, edge_pts, keeping):
    lower_ext = 2 * side_pts + (edge_pts if keeping else 0)
    starts = [(0, side_pts), (lower_ext, side_pts), (side_pts, side_pts), (lower_ext + side_pts, side_pts)]
    if keeping:
        starts = starts + [(2 * side_pts, edge_pts), (lower_ext + 2 * side_pts, edge_pts)]
    return [(start_at, start_at + length) for start_at, length in starts]

def merge_boxes(map_lower, map_upper, side_pts, edge_pts, keeping):
    blocks, solved = merge_setup(map_lower, map_upper, side_pts, edge_pts, keeping)
    merged = jnp.concatenate([rows_lower(blocks, solved), rows_upper(blocks, solved)], 1)
    span_list = order_spans(side_pts, edge_pts, keeping)
    return block_take(merged, span_list, span_list)

def subdomain_map(leaves):
    edge_pts = leaves.shape[-1] // 4
    lower_pair = merge_boxes(leaves[0], leaves[1], edge_pts, edge_pts, True)
    upper_pair = merge_boxes(leaves[2], leaves[3], edge_pts, edge_pts, True)
    return merge_boxes(lower_pair, upper_pair, 2 * edge_pts, edge_pts, False)

def incident(position, thetas, face_pts, edge_pts):
    heights = (jnp.arange(face_pts, dtype=jnp.float32) + 0.5) / edge_pts
    across_x = jnp.cos(thetas)[:, None]
    along_y = jnp.sin(thetas)[:, None]
    left_phase = wavenumber * (position * across_x + heights[None, :] * along_y)
    right_phase = wavenumber * ((position + 1.0) * across_x + heights[None, :] * along_y)
    phases = jnp.concatenate([left_phase, right_phase], 1)
    return jnp.stack([jnp.cos(phases), jnp.sin(phases)])

def reference(leaf_maps, angles):
    edge_pts = leaf_maps.shape[-1] // 4
    face_pts = leaf_maps.shape[1] * edge_pts
    angle_count = angles.shape[0]
    sub_count = leaf_maps.shape[0]

    def advance(carried, inputs):
        leaves, sub_index = inputs
        position = sub_index.astype(jnp.float32)
        incoming = incident(position, angles, face_pts, edge_pts)
        lefts = []
        rights = []
        for polarity in range(2):
            full_map = subdomain_map(leaves[:, polarity])
            driven = complex_apply(full_map, incoming)
            chained = carried[polarity]
            lefts.append(driven[:, :, :face_pts] + complex_apply(full_map[:, :face_pts, :face_pts], chained))
            rights.append(driven[:, :, face_pts:] + complex_apply(full_map[:, face_pts:, :face_pts], chained))
        right_all = jnp.stack(rights)
        return (right_all, (jnp.stack(lefts), right_all))
    start = jnp.zeros((2, 2, angle_count, face_pts), jnp.float32)
    unused, (left_out, right_out) = lax.scan(advance, start, (leaf_maps, jnp.arange(sub_count, dtype=jnp.int32)))

    def arrange(values):
        shaped = values.reshape(sub_count, 2, 2, 2, angle_count // 2, face_pts)
        return shaped.transpose(0, 2, 3, 1, 4, 5).reshape(sub_count, 2, 2 * angle_count, face_pts)
    return (arrange(left_out), arrange(right_out))
```

```python
import jax
import jax.numpy as jnp
from jax import lax
from jax.sharding import PartitionSpec as P

precise = lax.Precision.HIGHEST
wavenumber = 12.0


def from_partner(x, axis, apart):
    return lax.ppermute(x, axis, [(i, i ^ 1 << apart) for i in range(lax.axis_size(axis))])


def passed_along(x, axis, by):
    peers = lax.axis_size(axis)
    pairs = [(i, i + by) for i in range(peers) if 0 <= i + by < peers]
    return lax.ppermute(x, axis, pairs)


def plain_dot(left_mat, right_mat):
    return jnp.dot(left_mat, right_mat, precision=precise, preferred_element_type=jnp.float32)


def complex_dot(left_mat, right_mat):
    real_part = plain_dot(left_mat[0], right_mat[0]) - plain_dot(left_mat[1], right_mat[1])
    imag_part = plain_dot(left_mat[0], right_mat[1]) + plain_dot(left_mat[1], right_mat[0])
    return jnp.stack([real_part, imag_part])


def side_dot(vectors, matrix):
    return lax.dot_general(
        vectors,
        matrix,
        (((1,), (1,)), ((), ())),
        precision=precise,
        preferred_element_type=jnp.float32,
    )


def complex_apply(matrix, vectors):
    real_part = side_dot(vectors[0], matrix[0]) - side_dot(vectors[1], matrix[1])
    imag_part = side_dot(vectors[0], matrix[1]) + side_dot(vectors[1], matrix[0])
    return jnp.stack([real_part, imag_part])


def complex_solve(system, right_mat):
    size_n = system.shape[1]
    upper_band = jnp.concatenate([system[0], -system[1]], 1)
    lower_band = jnp.concatenate([system[1], system[0]], 1)
    big_mat = jnp.concatenate([upper_band, lower_band], 0)
    stacked = jnp.concatenate([right_mat[0], right_mat[1]], 0)
    normal = lax.dot_general(
        big_mat,
        big_mat,
        (((0,), (0,)), ((), ())),
        precision=precise,
        preferred_element_type=jnp.float32,
    )
    projected = lax.dot_general(
        big_mat,
        stacked,
        (((0,), (0,)), ((), ())),
        precision=precise,
        preferred_element_type=jnp.float32,
    )
    factor = jnp.linalg.cholesky(normal)
    solution = jax.scipy.linalg.cho_solve((factor, True), projected)
    return jnp.stack([solution[:size_n], solution[size_n:]])


def block_take(matrix, row_list, col_list):
    row_cat = jnp.concatenate([matrix[:, start_at:stop_at] for start_at, stop_at in row_list], 1)
    return jnp.concatenate([row_cat[:, :, start_at:stop_at] for start_at, stop_at in col_list], 2)


def merge_setup(map_lower, map_upper, side_pts, edge_pts, keeping):
    total_pts = 2 * side_pts + 2 * edge_pts
    lower_ext = 2 * side_pts + (edge_pts if keeping else 0)
    lower_outer = [(0, lower_ext)]
    lower_inner = [(2 * side_pts + edge_pts, total_pts)]
    upper_outer = [(0, 2 * side_pts)] + ([(2 * side_pts + edge_pts, total_pts)] if keeping else [])
    upper_inner = [(2 * side_pts, 2 * side_pts + edge_pts)]
    alpha_outer = block_take(map_lower, lower_outer, lower_outer)
    alpha_reach = block_take(map_lower, lower_outer, lower_inner)
    alpha_inward = block_take(map_lower, lower_inner, lower_outer)
    alpha_inner = block_take(map_lower, lower_inner, lower_inner)
    beta_outer = block_take(map_upper, upper_outer, upper_outer)
    beta_reach = block_take(map_upper, upper_outer, upper_inner)
    beta_inward = block_take(map_upper, upper_inner, upper_outer)
    beta_inner = block_take(map_upper, upper_inner, upper_inner)
    identity_mat = jnp.stack(
        [jnp.eye(edge_pts, dtype=jnp.float32), jnp.zeros((edge_pts, edge_pts), jnp.float32)]
    )
    system = identity_mat - complex_dot(beta_inner, alpha_inner)
    right_mat = jnp.concatenate([-complex_dot(beta_inner, alpha_inward), beta_inward], 2)
    solved = complex_solve(system, right_mat)
    blocks = (alpha_outer, alpha_reach, alpha_inward, alpha_inner, beta_outer, beta_reach)
    return (blocks, solved)


def rows_lower(blocks, solved):
    alpha_outer, alpha_reach = (blocks[0], blocks[1])
    upper_count = solved.shape[2] - alpha_outer.shape[2]
    padded = jnp.concatenate(
        [alpha_outer, jnp.zeros((2, alpha_outer.shape[1], upper_count), jnp.float32)], 2
    )
    return padded - complex_dot(alpha_reach, solved)


def rows_upper(blocks, solved):
    alpha_inward, alpha_inner, beta_outer, beta_reach = (blocks[2], blocks[3], blocks[4], blocks[5])
    leading = jnp.concatenate([-complex_dot(beta_reach, alpha_inward), beta_outer], 2)
    return leading + complex_dot(complex_dot(beta_reach, alpha_inner), solved)


def order_spans(side_pts, edge_pts, keeping):
    lower_ext = 2 * side_pts + (edge_pts if keeping else 0)
    starts = [
        (0, side_pts),
        (lower_ext, side_pts),
        (side_pts, side_pts),
        (lower_ext + side_pts, side_pts),
    ]
    if keeping:
        starts = starts + [(2 * side_pts, edge_pts), (lower_ext + 2 * side_pts, edge_pts)]
    return [(start_at, start_at + length) for start_at, length in starts]


def merge_boxes(map_lower, map_upper, side_pts, edge_pts, keeping):
    blocks, solved = merge_setup(map_lower, map_upper, side_pts, edge_pts, keeping)
    merged = jnp.concatenate([rows_lower(blocks, solved), rows_upper(blocks, solved)], 1)
    span_list = order_spans(side_pts, edge_pts, keeping)
    return block_take(merged, span_list, span_list)


def incident(position, thetas, face_pts, edge_pts):
    heights = (jnp.arange(face_pts, dtype=jnp.float32) + 0.5) / edge_pts
    across_x = jnp.cos(thetas)[:, None]
    along_y = jnp.sin(thetas)[:, None]
    left_phase = wavenumber * (position * across_x + heights[None, :] * along_y)
    right_phase = wavenumber * ((position + 1.0) * across_x + heights[None, :] * along_y)
    phases = jnp.concatenate([left_phase, right_phase], 1)
    return jnp.stack([jnp.cos(phases), jnp.sin(phases)])


def shifted_along(x, axis, pairs):
    return lax.ppermute(x, axis, pairs)


def trim_pair(paired, lower_two, side_pts, edge_pts):
    kept_lower = [(0, 2 * side_pts), (2 * side_pts + edge_pts, 2 * side_pts + 2 * edge_pts)]
    kept_upper = [(0, 2 * side_pts + edge_pts)]
    return jnp.where(
        lower_two,
        block_take(paired, kept_lower, kept_lower),
        block_take(paired, kept_upper, kept_upper),
    )


def untrim_pair(small, from_lower, side_pts, edge_pts):
    lead = 2 * side_pts
    zero_col = jnp.zeros((2, small.shape[1], edge_pts), jnp.float32)
    zero_row = jnp.zeros((2, edge_pts, small.shape[2] + edge_pts), jnp.float32)
    as_lower = jnp.concatenate([small[:, :, :lead], zero_col, small[:, :, lead:]], 2)
    as_lower = jnp.concatenate([as_lower[:, :lead], zero_row, as_lower[:, lead:]], 1)
    as_upper = jnp.concatenate([small, zero_col], 2)
    as_upper = jnp.concatenate([as_upper, zero_row], 1)
    return jnp.where(from_lower, as_lower, as_upper)


def per_device(leaf_maps, angles):
    edge_pts = leaf_maps.shape[-1] // 4
    leaf_id = lax.axis_index("leaf")
    pol_id = leaf_id % 2
    half_id = leaf_id // 2
    own_maps = leaf_maps[0, 0]
    own_pol = lax.dynamic_index_in_dim(own_maps, pol_id, 0, keepdims=False)
    other_pol = lax.dynamic_index_in_dim(own_maps, 1 - pol_id, 0, keepdims=False)
    partner = from_partner(other_pol, "leaf", 0)
    is_lower = pol_id == 0
    paired = merge_boxes(
        jnp.where(is_lower, own_pol, partner),
        jnp.where(is_lower, partner, own_pol),
        edge_pts,
        edge_pts,
        True,
    )
    lower_two = half_id == 0
    sent_pair = trim_pair(paired, lower_two, 2 * edge_pts, edge_pts)
    neighbor = untrim_pair(from_partner(sent_pair, "leaf", 1), jnp.logical_not(lower_two), 2 * edge_pts, edge_pts)
    map_lower = jnp.where(lower_two, paired, neighbor)
    map_upper = jnp.where(lower_two, neighbor, paired)
    full_map = merge_boxes(map_lower, map_upper, 2 * edge_pts, edge_pts, False)
    face_pts = full_map.shape[1] // 2
    col_count = angles.shape[0] // 2
    thetas = lax.dynamic_slice_in_dim(angles, half_id * col_count, col_count)
    wide_id = lax.axis_index("wide")
    wide_count = lax.axis_size("wide")
    position = wide_id.astype(jnp.float32)
    incoming = incident(position, thetas, face_pts, edge_pts)
    driven = complex_apply(full_map, incoming)
    transfer = full_map[:, face_pts:, :face_pts]
    outgoing = driven[:, :, face_pts:]
    blank = jnp.zeros_like(outgoing)

    to_odd = [(i, i + 1) for i in range(0, wide_count, 2)]
    handed = shifted_along(jnp.concatenate([transfer, outgoing], 1), "wide", to_odd)
    prev_transfer = handed[:, :face_pts]
    prev_outgoing = handed[:, face_pts:]
    double_map = complex_dot(transfer, prev_transfer)
    double_drive = outgoing + complex_apply(transfer, prev_outgoing)

    odd_pairs = [(i, i + 2) for i in range(1, wide_count - 2, 2)]

    def advance(step_at, stored):
        active = wide_id == 2 * step_at + 1
        sending = lax.cond(
            active, lambda: double_drive + complex_apply(double_map, stored), lambda: blank
        )
        received = shifted_along(sending, "wide", odd_pairs)
        return jnp.where(wide_id == 2 * step_at + 3, received, stored)

    even_in = lax.fori_loop(0, wide_count // 2 - 1, advance, blank)
    to_even = [(i + 1, i) for i in range(0, wide_count, 2)]
    given = shifted_along(even_in, "wide", to_even)
    is_odd = wide_id % 2 == 1
    odd_in = prev_outgoing + complex_apply(prev_transfer, even_in)
    chained = jnp.where(is_odd, odd_in, given)
    right_part = outgoing + complex_apply(transfer, chained)
    left_part = driven[:, :, :face_pts] + complex_apply(full_map[:, :face_pts, :face_pts], chained)
    return (left_part[None], right_part[None])


def solution(mesh):
    placed = (P("wide", "leaf", None, None, None, None), P())
    return jax.shard_map(
        per_device,
        mesh=mesh,
        in_specs=placed,
        out_specs=(P("wide", None, "leaf", None), P("wide", None, "leaf", None)),
        check_vma=False,
    )
```

```python
import jax
import jax.numpy as jnp
from jax import lax
from jax.sharding import PartitionSpec as P

precise = lax.Precision.HIGHEST
wavenumber = 12.0


def from_partner(x, axis, apart):
    return lax.ppermute(x, axis, [(i, i ^ 1 << apart) for i in range(lax.axis_size(axis))])


def passed_along(x, axis, by):
    peers = lax.axis_size(axis)
    pairs = [(i, i + by) for i in range(peers) if 0 <= i + by < peers]
    return lax.ppermute(x, axis, pairs)


def plain_dot(left_mat, right_mat):
    return jnp.dot(left_mat, right_mat, precision=precise, preferred_element_type=jnp.float32)


def complex_dot(left_mat, right_mat):
    real_part = plain_dot(left_mat[0], right_mat[0]) - plain_dot(left_mat[1], right_mat[1])
    imag_part = plain_dot(left_mat[0], right_mat[1]) + plain_dot(left_mat[1], right_mat[0])
    return jnp.stack([real_part, imag_part])


def side_dot(vectors, matrix):
    return lax.dot_general(
        vectors,
        matrix,
        (((1,), (1,)), ((), ())),
        precision=precise,
        preferred_element_type=jnp.float32,
    )


def complex_apply(matrix, vectors):
    real_part = side_dot(vectors[0], matrix[0]) - side_dot(vectors[1], matrix[1])
    imag_part = side_dot(vectors[0], matrix[1]) + side_dot(vectors[1], matrix[0])
    return jnp.stack([real_part, imag_part])


def complex_solve(system, right_mat):
    size_n = system.shape[1]
    upper_band = jnp.concatenate([system[0], -system[1]], 1)
    lower_band = jnp.concatenate([system[1], system[0]], 1)
    big_mat = jnp.concatenate([upper_band, lower_band], 0)
    stacked = jnp.concatenate([right_mat[0], right_mat[1]], 0)
    normal = lax.dot_general(
        big_mat,
        big_mat,
        (((0,), (0,)), ((), ())),
        precision=precise,
        preferred_element_type=jnp.float32,
    )
    projected = lax.dot_general(
        big_mat,
        stacked,
        (((0,), (0,)), ((), ())),
        precision=precise,
        preferred_element_type=jnp.float32,
    )
    factor = jnp.linalg.cholesky(normal)
    solution = jax.scipy.linalg.cho_solve((factor, True), projected)
    return jnp.stack([solution[:size_n], solution[size_n:]])


def block_take(matrix, row_list, col_list):
    row_cat = jnp.concatenate([matrix[:, start_at:stop_at] for start_at, stop_at in row_list], 1)
    return jnp.concatenate([row_cat[:, :, start_at:stop_at] for start_at, stop_at in col_list], 2)


def merge_setup(map_lower, map_upper, side_pts, edge_pts, keeping):
    total_pts = 2 * side_pts + 2 * edge_pts
    lower_ext = 2 * side_pts + (edge_pts if keeping else 0)
    lower_outer = [(0, lower_ext)]
    lower_inner = [(2 * side_pts + edge_pts, total_pts)]
    upper_outer = [(0, 2 * side_pts)] + ([(2 * side_pts + edge_pts, total_pts)] if keeping else [])
    upper_inner = [(2 * side_pts, 2 * side_pts + edge_pts)]
    alpha_outer = block_take(map_lower, lower_outer, lower_outer)
    alpha_reach = block_take(map_lower, lower_outer, lower_inner)
    alpha_inward = block_take(map_lower, lower_inner, lower_outer)
    alpha_inner = block_take(map_lower, lower_inner, lower_inner)
    beta_outer = block_take(map_upper, upper_outer, upper_outer)
    beta_reach = block_take(map_upper, upper_outer, upper_inner)
    beta_inward = block_take(map_upper, upper_inner, upper_outer)
    beta_inner = block_take(map_upper, upper_inner, upper_inner)
    identity_mat = jnp.stack(
        [jnp.eye(edge_pts, dtype=jnp.float32), jnp.zeros((edge_pts, edge_pts), jnp.float32)]
    )
    system = identity_mat - complex_dot(beta_inner, alpha_inner)
    right_mat = jnp.concatenate([-complex_dot(beta_inner, alpha_inward), beta_inward], 2)
    solved = complex_solve(system, right_mat)
    blocks = (alpha_outer, alpha_reach, alpha_inward, alpha_inner, beta_outer, beta_reach)
    return (blocks, solved)


def rows_lower(blocks, solved):
    alpha_outer, alpha_reach = (blocks[0], blocks[1])
    upper_count = solved.shape[2] - alpha_outer.shape[2]
    padded = jnp.concatenate(
        [alpha_outer, jnp.zeros((2, alpha_outer.shape[1], upper_count), jnp.float32)], 2
    )
    return padded - complex_dot(alpha_reach, solved)


def rows_upper(blocks, solved):
    alpha_inward, alpha_inner, beta_outer, beta_reach = (blocks[2], blocks[3], blocks[4], blocks[5])
    leading = jnp.concatenate([-complex_dot(beta_reach, alpha_inward), beta_outer], 2)
    return leading + complex_dot(complex_dot(beta_reach, alpha_inner), solved)


def order_spans(side_pts, edge_pts, keeping):
    lower_ext = 2 * side_pts + (edge_pts if keeping else 0)
    starts = [
        (0, side_pts),
        (lower_ext, side_pts),
        (side_pts, side_pts),
        (lower_ext + side_pts, side_pts),
    ]
    if keeping:
        starts = starts + [(2 * side_pts, edge_pts), (lower_ext + 2 * side_pts, edge_pts)]
    return [(start_at, start_at + length) for start_at, length in starts]


def merge_boxes(map_lower, map_upper, side_pts, edge_pts, keeping):
    blocks, solved = merge_setup(map_lower, map_upper, side_pts, edge_pts, keeping)
    merged = jnp.concatenate([rows_lower(blocks, solved), rows_upper(blocks, solved)], 1)
    span_list = order_spans(side_pts, edge_pts, keeping)
    return block_take(merged, span_list, span_list)


def incident(position, thetas, face_pts, edge_pts):
    heights = (jnp.arange(face_pts, dtype=jnp.float32) + 0.5) / edge_pts
    across_x = jnp.cos(thetas)[:, None]
    along_y = jnp.sin(thetas)[:, None]
    left_phase = wavenumber * (position * across_x + heights[None, :] * along_y)
    right_phase = wavenumber * ((position + 1.0) * across_x + heights[None, :] * along_y)
    phases = jnp.concatenate([left_phase, right_phase], 1)
    return jnp.stack([jnp.cos(phases), jnp.sin(phases)])


def shifted_along(x, axis, pairs):
    return lax.ppermute(x, axis, pairs)


def role_spans(side_pts, edge_pts, keeping, lower):
    total_pts = 2 * side_pts + 2 * edge_pts
    if lower:
        outer = [(0, 2 * side_pts + (edge_pts if keeping else 0))]
        inner = [(2 * side_pts + edge_pts, total_pts)]
    else:
        outer = [(0, 2 * side_pts)] + ([(2 * side_pts + edge_pts, total_pts)] if keeping else [])
        inner = [(2 * side_pts, 2 * side_pts + edge_pts)]
    return outer, inner


def split_map(matrix, side_pts, edge_pts, keeping, lower):
    outer, inner = role_spans(side_pts, edge_pts, keeping, lower)
    cols = outer + inner
    return block_take(matrix, inner, cols), block_take(matrix, outer, cols)


def merge_parts(lower_in, lower_out, upper_in, upper_out, side_pts, edge_pts, keeping):
    n_ao = lower_out.shape[1]
    n_bo = upper_out.shape[1]
    alpha_outer = lower_out[:, :, :n_ao]
    alpha_reach = lower_out[:, :, n_ao:]
    alpha_inward = lower_in[:, :, :n_ao]
    alpha_inner = lower_in[:, :, n_ao:]
    beta_outer = upper_out[:, :, :n_bo]
    beta_reach = upper_out[:, :, n_bo:]
    beta_inward = upper_in[:, :, :n_bo]
    beta_inner = upper_in[:, :, n_bo:]
    identity_mat = jnp.stack(
        [jnp.eye(edge_pts, dtype=jnp.float32), jnp.zeros((edge_pts, edge_pts), jnp.float32)]
    )
    system = identity_mat - complex_dot(beta_inner, alpha_inner)
    right_mat = jnp.concatenate([-complex_dot(beta_inner, alpha_inward), beta_inward], 2)
    solved = complex_solve(system, right_mat)
    blocks = (alpha_outer, alpha_reach, alpha_inward, alpha_inner, beta_outer, beta_reach)
    merged = jnp.concatenate([rows_lower(blocks, solved), rows_upper(blocks, solved)], 1)
    span_list = order_spans(side_pts, edge_pts, keeping)
    return block_take(merged, span_list, span_list)


def exchange_merge(own, spare, own_is_lower, axis, apart, side_pts, edge_pts, keeping):
    spare_lo = split_map(spare, side_pts, edge_pts, keeping, True)
    spare_up = split_map(spare, side_pts, edge_pts, keeping, False)
    send_in = jnp.where(own_is_lower, spare_lo[0], spare_up[0])
    send_out = jnp.where(own_is_lower, spare_lo[1], spare_up[1])
    got_in = from_partner(send_in, axis, apart)
    got_out = from_partner(send_out, axis, apart)
    own_lo = split_map(own, side_pts, edge_pts, keeping, True)
    own_up = split_map(own, side_pts, edge_pts, keeping, False)
    lower_in = jnp.where(own_is_lower, own_lo[0], got_in)
    lower_out = jnp.where(own_is_lower, own_lo[1], got_out)
    upper_in = jnp.where(own_is_lower, got_in, own_up[0])
    upper_out = jnp.where(own_is_lower, got_out, own_up[1])
    return merge_parts(lower_in, lower_out, upper_in, upper_out, side_pts, edge_pts, keeping)


def real_block(matrix):
    return jnp.concatenate(
        [
            jnp.concatenate([matrix[0].T, matrix[1].T], 1),
            jnp.concatenate([-matrix[1].T, matrix[0].T], 1),
        ],
        0,
    )


def per_device(leaf_maps, angles):
    edge_pts = leaf_maps.shape[-1] // 4
    leaf_id = lax.axis_index("leaf")
    pol_id = leaf_id % 2
    half_id = leaf_id // 2
    own_maps = leaf_maps[0, 0]
    own_pol = lax.dynamic_index_in_dim(own_maps, pol_id, 0, keepdims=False)
    other_pol = lax.dynamic_index_in_dim(own_maps, 1 - pol_id, 0, keepdims=False)
    paired = exchange_merge(own_pol, other_pol, pol_id == 0, "leaf", 0, edge_pts, edge_pts, True)
    full_map = exchange_merge(paired, paired, half_id == 0, "leaf", 1, 2 * edge_pts, edge_pts, False)
    face_pts = full_map.shape[1] // 2
    col_count = angles.shape[0] // 2
    thetas = lax.dynamic_slice_in_dim(angles, half_id * col_count, col_count)
    wide_id = lax.axis_index("wide")
    wide_count = lax.axis_size("wide")
    position = wide_id.astype(jnp.float32)
    incoming = incident(position, thetas, face_pts, edge_pts)
    driven = complex_apply(full_map, incoming)
    transfer = full_map[:, face_pts:, :face_pts]
    outgoing = driven[:, :, face_pts:]

    to_odd = [(i, i + 1) for i in range(0, wide_count, 2)]
    handed = shifted_along(jnp.concatenate([transfer, outgoing], 1), "wide", to_odd)
    prev_transfer = handed[:, :face_pts]
    prev_outgoing = handed[:, face_pts:]
    double_map = real_block(complex_dot(transfer, prev_transfer))
    double_drive = outgoing + complex_apply(transfer, prev_outgoing)
    flat_drive = jnp.concatenate([double_drive[0], double_drive[1]], 1)
    blank = jnp.zeros_like(flat_drive)

    odd_pairs = [(i, i + 2) for i in range(1, wide_count - 2, 2)]

    def advance(step_at, stored):
        active = wide_id == 2 * step_at + 1
        sending = lax.cond(
            active,
            lambda: flat_drive
            + jnp.dot(stored, double_map, precision=lax.Precision.HIGH, preferred_element_type=jnp.float32),
            lambda: blank,
        )
        received = shifted_along(sending, "wide", odd_pairs)
        return jnp.where(wide_id == 2 * step_at + 3, received, stored)

    flat_in = lax.fori_loop(0, wide_count // 2 - 1, advance, blank)
    even_in = jnp.stack([flat_in[:, :face_pts], flat_in[:, face_pts:]])
    to_even = [(i + 1, i) for i in range(0, wide_count, 2)]
    given = shifted_along(even_in, "wide", to_even)
    is_odd = wide_id % 2 == 1
    odd_in = prev_outgoing + complex_apply(prev_transfer, even_in)
    chained = jnp.where(is_odd, odd_in, given)
    right_part = outgoing + complex_apply(transfer, chained)
    left_part = driven[:, :, :face_pts] + complex_apply(full_map[:, :face_pts, :face_pts], chained)
    return (left_part[None], right_part[None])


def solution(mesh):
    placed = (P("wide", "leaf", None, None, None, None), P())
    return jax.shard_map(
        per_device,
        mesh=mesh,
        in_specs=placed,
        out_specs=(P("wide", None, "leaf", None), P("wide", None, "leaf", None)),
        check_vma=False,
    )
```

```python
import jax
import jax.numpy as jnp
from jax import lax
from jax.sharding import PartitionSpec as P

precise = lax.Precision.HIGHEST
wavenumber = 12.0


def from_partner(x, axis, apart):
    return lax.ppermute(x, axis, [(i, i ^ 1 << apart) for i in range(lax.axis_size(axis))])


def passed_along(x, axis, by):
    peers = lax.axis_size(axis)
    pairs = [(i, i + by) for i in range(peers) if 0 <= i + by < peers]
    return lax.ppermute(x, axis, pairs)


def plain_dot(left_mat, right_mat):
    return jnp.dot(left_mat, right_mat, precision=precise, preferred_element_type=jnp.float32)


def complex_dot(left_mat, right_mat):
    real_part = plain_dot(left_mat[0], right_mat[0]) - plain_dot(left_mat[1], right_mat[1])
    imag_part = plain_dot(left_mat[0], right_mat[1]) + plain_dot(left_mat[1], right_mat[0])
    return jnp.stack([real_part, imag_part])


def side_dot(vectors, matrix):
    return lax.dot_general(
        vectors,
        matrix,
        (((1,), (1,)), ((), ())),
        precision=precise,
        preferred_element_type=jnp.float32,
    )


def complex_apply(matrix, vectors):
    real_part = side_dot(vectors[0], matrix[0]) - side_dot(vectors[1], matrix[1])
    imag_part = side_dot(vectors[0], matrix[1]) + side_dot(vectors[1], matrix[0])
    return jnp.stack([real_part, imag_part])


def complex_solve(system, right_mat):
    size_n = system.shape[1]
    upper_band = jnp.concatenate([system[0], -system[1]], 1)
    lower_band = jnp.concatenate([system[1], system[0]], 1)
    big_mat = jnp.concatenate([upper_band, lower_band], 0)
    stacked = jnp.concatenate([right_mat[0], right_mat[1]], 0)
    normal = lax.dot_general(
        big_mat,
        big_mat,
        (((0,), (0,)), ((), ())),
        precision=precise,
        preferred_element_type=jnp.float32,
    )
    projected = lax.dot_general(
        big_mat,
        stacked,
        (((0,), (0,)), ((), ())),
        precision=precise,
        preferred_element_type=jnp.float32,
    )
    factor = jnp.linalg.cholesky(normal)
    solution = jax.scipy.linalg.cho_solve((factor, True), projected)
    return jnp.stack([solution[:size_n], solution[size_n:]])


def block_take(matrix, row_list, col_list):
    row_cat = jnp.concatenate([matrix[:, start_at:stop_at] for start_at, stop_at in row_list], 1)
    return jnp.concatenate([row_cat[:, :, start_at:stop_at] for start_at, stop_at in col_list], 2)


def merge_setup(map_lower, map_upper, side_pts, edge_pts, keeping):
    total_pts = 2 * side_pts + 2 * edge_pts
    lower_ext = 2 * side_pts + (edge_pts if keeping else 0)
    lower_outer = [(0, lower_ext)]
    lower_inner = [(2 * side_pts + edge_pts, total_pts)]
    upper_outer = [(0, 2 * side_pts)] + ([(2 * side_pts + edge_pts, total_pts)] if keeping else [])
    upper_inner = [(2 * side_pts, 2 * side_pts + edge_pts)]
    alpha_outer = block_take(map_lower, lower_outer, lower_outer)
    alpha_reach = block_take(map_lower, lower_outer, lower_inner)
    alpha_inward = block_take(map_lower, lower_inner, lower_outer)
    alpha_inner = block_take(map_lower, lower_inner, lower_inner)
    beta_outer = block_take(map_upper, upper_outer, upper_outer)
    beta_reach = block_take(map_upper, upper_outer, upper_inner)
    beta_inward = block_take(map_upper, upper_inner, upper_outer)
    beta_inner = block_take(map_upper, upper_inner, upper_inner)
    identity_mat = jnp.stack(
        [jnp.eye(edge_pts, dtype=jnp.float32), jnp.zeros((edge_pts, edge_pts), jnp.float32)]
    )
    system = identity_mat - complex_dot(beta_inner, alpha_inner)
    right_mat = jnp.concatenate([-complex_dot(beta_inner, alpha_inward), beta_inward], 2)
    solved = complex_solve(system, right_mat)
    blocks = (alpha_outer, alpha_reach, alpha_inward, alpha_inner, beta_outer, beta_reach)
    return (blocks, solved)


def rows_lower(blocks, solved):
    alpha_outer, alpha_reach = (blocks[0], blocks[1])
    upper_count = solved.shape[2] - alpha_outer.shape[2]
    padded = jnp.concatenate(
        [alpha_outer, jnp.zeros((2, alpha_outer.shape[1], upper_count), jnp.float32)], 2
    )
    return padded - complex_dot(alpha_reach, solved)


def rows_upper(blocks, solved):
    alpha_inward, alpha_inner, beta_outer, beta_reach = (blocks[2], blocks[3], blocks[4], blocks[5])
    leading = jnp.concatenate([-complex_dot(beta_reach, alpha_inward), beta_outer], 2)
    return leading + complex_dot(complex_dot(beta_reach, alpha_inner), solved)


def order_spans(side_pts, edge_pts, keeping):
    lower_ext = 2 * side_pts + (edge_pts if keeping else 0)
    starts = [
        (0, side_pts),
        (lower_ext, side_pts),
        (side_pts, side_pts),
        (lower_ext + side_pts, side_pts),
    ]
    if keeping:
        starts = starts + [(2 * side_pts, edge_pts), (lower_ext + 2 * side_pts, edge_pts)]
    return [(start_at, start_at + length) for start_at, length in starts]


def merge_boxes(map_lower, map_upper, side_pts, edge_pts, keeping):
    blocks, solved = merge_setup(map_lower, map_upper, side_pts, edge_pts, keeping)
    merged = jnp.concatenate([rows_lower(blocks, solved), rows_upper(blocks, solved)], 1)
    span_list = order_spans(side_pts, edge_pts, keeping)
    return block_take(merged, span_list, span_list)


def incident(position, thetas, face_pts, edge_pts):
    heights = (jnp.arange(face_pts, dtype=jnp.float32) + 0.5) / edge_pts
    across_x = jnp.cos(thetas)[:, None]
    along_y = jnp.sin(thetas)[:, None]
    left_phase = wavenumber * (position * across_x + heights[None, :] * along_y)
    right_phase = wavenumber * ((position + 1.0) * across_x + heights[None, :] * along_y)
    phases = jnp.concatenate([left_phase, right_phase], 1)
    return jnp.stack([jnp.cos(phases), jnp.sin(phases)])


def shifted_along(x, axis, pairs):
    return lax.ppermute(x, axis, pairs)


def role_spans(side_pts, edge_pts, keeping, lower):
    total_pts = 2 * side_pts + 2 * edge_pts
    if lower:
        outer = [(0, 2 * side_pts + (edge_pts if keeping else 0))]
        inner = [(2 * side_pts + edge_pts, total_pts)]
    else:
        outer = [(0, 2 * side_pts)] + ([(2 * side_pts + edge_pts, total_pts)] if keeping else [])
        inner = [(2 * side_pts, 2 * side_pts + edge_pts)]
    return outer, inner


def split_map(matrix, side_pts, edge_pts, keeping, lower):
    outer, inner = role_spans(side_pts, edge_pts, keeping, lower)
    cols = outer + inner
    return block_take(matrix, inner, cols), block_take(matrix, outer, cols)


def merge_parts(lower_in, lower_out, upper_in, upper_out, side_pts, edge_pts, keeping):
    n_ao = lower_out.shape[1]
    n_bo = upper_out.shape[1]
    alpha_outer = lower_out[:, :, :n_ao]
    alpha_reach = lower_out[:, :, n_ao:]
    alpha_inward = lower_in[:, :, :n_ao]
    alpha_inner = lower_in[:, :, n_ao:]
    beta_outer = upper_out[:, :, :n_bo]
    beta_reach = upper_out[:, :, n_bo:]
    beta_inward = upper_in[:, :, :n_bo]
    beta_inner = upper_in[:, :, n_bo:]
    identity_mat = jnp.stack(
        [jnp.eye(edge_pts, dtype=jnp.float32), jnp.zeros((edge_pts, edge_pts), jnp.float32)]
    )
    system = identity_mat - complex_dot(beta_inner, alpha_inner)
    right_mat = jnp.concatenate([-complex_dot(beta_inner, alpha_inward), beta_inward], 2)
    solved = complex_solve(system, right_mat)
    blocks = (alpha_outer, alpha_reach, alpha_inward, alpha_inner, beta_outer, beta_reach)
    merged = jnp.concatenate([rows_lower(blocks, solved), rows_upper(blocks, solved)], 1)
    span_list = order_spans(side_pts, edge_pts, keeping)
    return block_take(merged, span_list, span_list)


def exchange_merge(own, spare, own_is_lower, axis, apart, side_pts, edge_pts, keeping):
    spare_lo = split_map(spare, side_pts, edge_pts, keeping, True)
    spare_up = split_map(spare, side_pts, edge_pts, keeping, False)
    send_in = jnp.where(own_is_lower, spare_lo[0], spare_up[0])
    send_out = jnp.where(own_is_lower, spare_lo[1], spare_up[1])
    got_in = from_partner(send_in, axis, apart)
    got_in, send_out = lax.optimization_barrier((got_in, send_out))
    got_out = from_partner(send_out, axis, apart)
    own_lo = split_map(own, side_pts, edge_pts, keeping, True)
    own_up = split_map(own, side_pts, edge_pts, keeping, False)
    lower_in = jnp.where(own_is_lower, own_lo[0], got_in)
    lower_out = jnp.where(own_is_lower, own_lo[1], got_out)
    upper_in = jnp.where(own_is_lower, got_in, own_up[0])
    upper_out = jnp.where(own_is_lower, got_out, own_up[1])
    return merge_parts(lower_in, lower_out, upper_in, upper_out, side_pts, edge_pts, keeping)


def real_block(matrix):
    return jnp.concatenate(
        [
            jnp.concatenate([matrix[0].T, matrix[1].T], 1),
            jnp.concatenate([-matrix[1].T, matrix[0].T], 1),
        ],
        0,
    )


def per_device(leaf_maps, angles):
    edge_pts = leaf_maps.shape[-1] // 4
    leaf_id = lax.axis_index("leaf")
    pol_id = leaf_id % 2
    half_id = leaf_id // 2
    own_maps = leaf_maps[0, 0]
    own_pol = lax.dynamic_index_in_dim(own_maps, pol_id, 0, keepdims=False)
    other_pol = lax.dynamic_index_in_dim(own_maps, 1 - pol_id, 0, keepdims=False)
    paired = exchange_merge(own_pol, other_pol, pol_id == 0, "leaf", 0, edge_pts, edge_pts, True)
    full_map = exchange_merge(paired, paired, half_id == 0, "leaf", 1, 2 * edge_pts, edge_pts, False)
    face_pts = full_map.shape[1] // 2
    col_count = angles.shape[0] // 2
    thetas = lax.dynamic_slice_in_dim(angles, half_id * col_count, col_count)
    wide_id = lax.axis_index("wide")
    wide_count = lax.axis_size("wide")
    position = wide_id.astype(jnp.float32)
    incoming = incident(position, thetas, face_pts, edge_pts)
    driven = complex_apply(full_map, incoming)
    transfer = full_map[:, face_pts:, :face_pts]
    outgoing = driven[:, :, face_pts:]

    to_odd = [(i, i + 1) for i in range(0, wide_count, 2)]
    handed = shifted_along(jnp.concatenate([transfer, outgoing], 1), "wide", to_odd)
    prev_transfer = handed[:, :face_pts]
    prev_outgoing = handed[:, face_pts:]
    double_map = complex_dot(transfer, prev_transfer)
    double_drive = outgoing + complex_apply(transfer, prev_outgoing)
    to_quad = [(i, i + 2) for i in range(1, wide_count, 4)]
    handed2 = shifted_along(jnp.concatenate([double_map, double_drive], 1), "wide", to_quad)
    prev_double_map = handed2[:, :face_pts]
    prev_double_drive = handed2[:, face_pts:]
    quad_map = real_block(complex_dot(double_map, prev_double_map))
    quad_drive = double_drive + complex_apply(double_map, prev_double_drive)
    flat_drive = jnp.concatenate([quad_drive[0], quad_drive[1]], 1)
    blank = jnp.zeros_like(flat_drive)

    quad_pairs = [(i, i + 4) for i in range(3, wide_count - 4, 4)]

    def advance(step_at, stored):
        active = wide_id == 4 * step_at + 3
        sending = lax.cond(
            active,
            lambda: flat_drive
            + jnp.dot(stored, quad_map, precision=lax.Precision.HIGH, preferred_element_type=jnp.float32),
            lambda: blank,
        )
        received = shifted_along(sending, "wide", quad_pairs)
        return jnp.where(wide_id == 4 * step_at + 7, received, stored)

    flat_in = lax.fori_loop(0, wide_count // 4 - 1, advance, blank)
    quad_in = jnp.stack([flat_in[:, :face_pts], flat_in[:, face_pts:]])
    back_pairs = [(i + 2, i) for i in range(1, wide_count, 4)]
    given2 = shifted_along(quad_in, "wide", back_pairs)
    own_next = prev_double_drive + complex_apply(prev_double_map, quad_in)
    even_in = jnp.where(wide_id % 4 == 3, own_next, given2)
    to_even = [(i + 1, i) for i in range(0, wide_count, 2)]
    given = shifted_along(even_in, "wide", to_even)
    is_odd = wide_id % 2 == 1
    odd_in = prev_outgoing + complex_apply(prev_transfer, even_in)
    chained = jnp.where(is_odd, odd_in, given)
    right_part = outgoing + complex_apply(transfer, chained)
    left_part = driven[:, :, :face_pts] + complex_apply(full_map[:, :face_pts, :face_pts], chained)
    return (left_part[None], right_part[None])


def solution(mesh):
    placed = (P("wide", "leaf", None, None, None, None), P())
    return jax.shard_map(
        per_device,
        mesh=mesh,
        in_specs=placed,
        out_specs=(P("wide", None, "leaf", None), P("wide", None, "leaf", None)),
        check_vma=False,
    )
```

```python
import jax
import jax.numpy as jnp
from jax import lax
from jax.sharding import PartitionSpec as P

precise = lax.Precision.HIGHEST
wavenumber = 12.0


def from_partner(x, axis, apart):
    return lax.ppermute(x, axis, [(i, i ^ 1 << apart) for i in range(lax.axis_size(axis))])


def plain_dot(left_mat, right_mat):
    return jnp.dot(left_mat, right_mat, precision=precise, preferred_element_type=jnp.float32)


def complex_dot(left_mat, right_mat):
    real_part = plain_dot(left_mat[0], right_mat[0]) - plain_dot(left_mat[1], right_mat[1])
    imag_part = plain_dot(left_mat[0], right_mat[1]) + plain_dot(left_mat[1], right_mat[0])
    return jnp.stack([real_part, imag_part])


def side_dot(vectors, matrix):
    return lax.dot_general(
        vectors,
        matrix,
        (((1,), (1,)), ((), ())),
        precision=precise,
        preferred_element_type=jnp.float32,
    )


def complex_apply(matrix, vectors):
    real_part = side_dot(vectors[0], matrix[0]) - side_dot(vectors[1], matrix[1])
    imag_part = side_dot(vectors[0], matrix[1]) + side_dot(vectors[1], matrix[0])
    return jnp.stack([real_part, imag_part])


def complex_solve(system, right_mat):
    size_n = system.shape[1]
    upper_band = jnp.concatenate([system[0], -system[1]], 1)
    lower_band = jnp.concatenate([system[1], system[0]], 1)
    big_mat = jnp.concatenate([upper_band, lower_band], 0)
    stacked = jnp.concatenate([right_mat[0], right_mat[1]], 0)
    normal = lax.dot_general(
        big_mat,
        big_mat,
        (((0,), (0,)), ((), ())),
        precision=precise,
        preferred_element_type=jnp.float32,
    )
    projected = lax.dot_general(
        big_mat,
        stacked,
        (((0,), (0,)), ((), ())),
        precision=precise,
        preferred_element_type=jnp.float32,
    )
    factor = jnp.linalg.cholesky(normal)
    solution = jax.scipy.linalg.cho_solve((factor, True), projected)
    return jnp.stack([solution[:size_n], solution[size_n:]])


def block_take(matrix, row_list, col_list):
    row_cat = jnp.concatenate([matrix[:, start_at:stop_at] for start_at, stop_at in row_list], 1)
    return jnp.concatenate([row_cat[:, :, start_at:stop_at] for start_at, stop_at in col_list], 2)


def rows_lower(blocks, solved):
    alpha_outer, alpha_reach = (blocks[0], blocks[1])
    upper_count = solved.shape[2] - alpha_outer.shape[2]
    padded = jnp.concatenate(
        [alpha_outer, jnp.zeros((2, alpha_outer.shape[1], upper_count), jnp.float32)], 2
    )
    return padded - complex_dot(alpha_reach, solved)


def rows_upper(blocks, solved):
    alpha_inward, alpha_inner, beta_outer, beta_reach = (blocks[2], blocks[3], blocks[4], blocks[5])
    leading = jnp.concatenate([-complex_dot(beta_reach, alpha_inward), beta_outer], 2)
    return leading + complex_dot(complex_dot(beta_reach, alpha_inner), solved)


def order_spans(side_pts, edge_pts, keeping):
    lower_ext = 2 * side_pts + (edge_pts if keeping else 0)
    starts = [
        (0, side_pts),
        (lower_ext, side_pts),
        (side_pts, side_pts),
        (lower_ext + side_pts, side_pts),
    ]
    if keeping:
        starts = starts + [(2 * side_pts, edge_pts), (lower_ext + 2 * side_pts, edge_pts)]
    return [(start_at, start_at + length) for start_at, length in starts]


def incident(position, thetas, face_pts, edge_pts):
    heights = (jnp.arange(face_pts, dtype=jnp.float32) + 0.5) / edge_pts
    across_x = jnp.cos(thetas)[:, None]
    along_y = jnp.sin(thetas)[:, None]
    left_phase = wavenumber * (position * across_x + heights[None, :] * along_y)
    right_phase = wavenumber * ((position + 1.0) * across_x + heights[None, :] * along_y)
    phases = jnp.concatenate([left_phase, right_phase], 1)
    return jnp.stack([jnp.cos(phases), jnp.sin(phases)])


def shifted_along(x, axis, pairs):
    return lax.ppermute(x, axis, pairs)


def role_spans(side_pts, edge_pts, keeping, lower):
    total_pts = 2 * side_pts + 2 * edge_pts
    if lower:
        outer = [(0, 2 * side_pts + (edge_pts if keeping else 0))]
        inner = [(2 * side_pts + edge_pts, total_pts)]
    else:
        outer = [(0, 2 * side_pts)] + ([(2 * side_pts + edge_pts, total_pts)] if keeping else [])
        inner = [(2 * side_pts, 2 * side_pts + edge_pts)]
    return outer, inner


def split_map(matrix, side_pts, edge_pts, keeping, lower):
    outer, inner = role_spans(side_pts, edge_pts, keeping, lower)
    cols = outer + inner
    return block_take(matrix, inner, cols), block_take(matrix, outer, cols)


def merge_parts(lower_in, lower_out, upper_in, upper_out, side_pts, edge_pts, keeping):
    n_ao = lower_out.shape[1]
    n_bo = upper_out.shape[1]
    alpha_outer = lower_out[:, :, :n_ao]
    alpha_reach = lower_out[:, :, n_ao:]
    alpha_inward = lower_in[:, :, :n_ao]
    alpha_inner = lower_in[:, :, n_ao:]
    beta_outer = upper_out[:, :, :n_bo]
    beta_reach = upper_out[:, :, n_bo:]
    beta_inward = upper_in[:, :, :n_bo]
    beta_inner = upper_in[:, :, n_bo:]
    identity_mat = jnp.stack(
        [jnp.eye(edge_pts, dtype=jnp.float32), jnp.zeros((edge_pts, edge_pts), jnp.float32)]
    )
    system = identity_mat - complex_dot(beta_inner, alpha_inner)
    right_mat = jnp.concatenate([-complex_dot(beta_inner, alpha_inward), beta_inward], 2)
    solved = complex_solve(system, right_mat)
    blocks = (alpha_outer, alpha_reach, alpha_inward, alpha_inner, beta_outer, beta_reach)
    merged = jnp.concatenate([rows_lower(blocks, solved), rows_upper(blocks, solved)], 1)
    span_list = order_spans(side_pts, edge_pts, keeping)
    return block_take(merged, span_list, span_list)


def exchange_merge(own, spare, own_is_lower, axis, apart, side_pts, edge_pts, keeping):
    spare_lo = split_map(spare, side_pts, edge_pts, keeping, True)
    spare_up = split_map(spare, side_pts, edge_pts, keeping, False)
    send_in = jnp.where(own_is_lower, spare_lo[0], spare_up[0])
    send_out = jnp.where(own_is_lower, spare_lo[1], spare_up[1])
    got_in = from_partner(send_in, axis, apart)
    got_in, send_out = lax.optimization_barrier((got_in, send_out))
    got_out = from_partner(send_out, axis, apart)
    own_lo = split_map(own, side_pts, edge_pts, keeping, True)
    own_up = split_map(own, side_pts, edge_pts, keeping, False)
    lower_in = jnp.where(own_is_lower, own_lo[0], got_in)
    lower_out = jnp.where(own_is_lower, own_lo[1], got_out)
    upper_in = jnp.where(own_is_lower, got_in, own_up[0])
    upper_out = jnp.where(own_is_lower, got_out, own_up[1])
    return merge_parts(lower_in, lower_out, upper_in, upper_out, side_pts, edge_pts, keeping)


def real_block(matrix):
    return jnp.concatenate(
        [
            jnp.concatenate([matrix[0].T, matrix[1].T], 1),
            jnp.concatenate([-matrix[1].T, matrix[0].T], 1),
        ],
        0,
    )


def per_device_body(leaf_maps, angles):
    edge_pts = leaf_maps.shape[-1] // 4
    leaf_id = lax.axis_index("leaf")
    pol_id = leaf_id % 2
    half_id = leaf_id // 2
    own_maps = leaf_maps[0, 0]
    own_pol = lax.dynamic_index_in_dim(own_maps, pol_id, 0, keepdims=False)
    other_pol = lax.dynamic_index_in_dim(own_maps, 1 - pol_id, 0, keepdims=False)
    paired = exchange_merge(own_pol, other_pol, pol_id == 0, "leaf", 0, edge_pts, edge_pts, True)
    full_map = exchange_merge(paired, paired, half_id == 0, "leaf", 1, 2 * edge_pts, edge_pts, False)
    face_pts = full_map.shape[1] // 2
    col_count = angles.shape[0] // 2
    thetas = lax.dynamic_slice_in_dim(angles, half_id * col_count, col_count)
    wide_id = lax.axis_index("wide")
    wide_count = lax.axis_size("wide")
    position = wide_id.astype(jnp.float32)
    incoming = incident(position, thetas, face_pts, edge_pts)
    driven = complex_apply(full_map, incoming)
    transfer = full_map[:, face_pts:, :face_pts]
    outgoing = driven[:, :, face_pts:]

    to_odd = [(i, i + 1) for i in range(0, wide_count, 2)]
    handed = shifted_along(jnp.concatenate([transfer, outgoing], 1), "wide", to_odd)
    prev_transfer = handed[:, :face_pts]
    prev_outgoing = handed[:, face_pts:]
    double_map = complex_dot(transfer, prev_transfer)
    double_drive = outgoing + complex_apply(transfer, prev_outgoing)
    to_quad = [(i, i + 2) for i in range(1, wide_count, 4)]
    handed2 = shifted_along(jnp.concatenate([double_map, double_drive], 1), "wide", to_quad)
    prev_double_map = handed2[:, :face_pts]
    prev_double_drive = handed2[:, face_pts:]
    quad_map = real_block(complex_dot(double_map, prev_double_map))
    quad_drive = double_drive + complex_apply(double_map, prev_double_drive)
    flat_drive = jnp.concatenate([quad_drive[0], quad_drive[1]], 1)
    blank = jnp.zeros_like(flat_drive)

    quad_pairs = [(i, i + 4) for i in range(3, wide_count - 4, 4)]

    def advance(step_at, stored):
        active = wide_id == 4 * step_at + 3
        sending = lax.cond(
            active,
            lambda: flat_drive
            + jnp.dot(stored, quad_map, precision=lax.Precision.HIGH, preferred_element_type=jnp.float32),
            lambda: blank,
        )
        received = shifted_along(sending, "wide", quad_pairs)
        return jnp.where(wide_id == 4 * step_at + 7, received, stored)

    flat_in = lax.fori_loop(0, wide_count // 4 - 1, advance, blank)
    quad_in = jnp.stack([flat_in[:, :face_pts], flat_in[:, face_pts:]])
    back_pairs = [(i + 2, i) for i in range(1, wide_count, 4)]
    given2 = shifted_along(quad_in, "wide", back_pairs)
    own_next = prev_double_drive + complex_apply(prev_double_map, quad_in)
    even_in = jnp.where(wide_id % 4 == 3, own_next, given2)
    to_even = [(i + 1, i) for i in range(0, wide_count, 2)]
    given = shifted_along(even_in, "wide", to_even)
    is_odd = wide_id % 2 == 1
    odd_in = prev_outgoing + complex_apply(prev_transfer, even_in)
    chained = jnp.where(is_odd, odd_in, given)
    right_part = outgoing + complex_apply(transfer, chained)
    left_part = driven[:, :, :face_pts] + complex_apply(full_map[:, :face_pts, :face_pts], chained)
    return (left_part[None], right_part[None])


def solution(mesh):
    placed = (P("wide", "leaf", None, None, None, None), P())
    return jax.shard_map(
        per_device_body,
        mesh=mesh,
        in_specs=placed,
        out_specs=(P("wide", None, "leaf", None), P("wide", None, "leaf", None)),
        check_vma=False,
    )
```

```python
import jax
import jax.numpy as jnp
from jax import lax
from jax.sharding import PartitionSpec as P

precise = lax.Precision.HIGHEST
quick = lax.Precision.HIGH
wavenumber = 12.0


def from_partner(x, axis, apart):
    return lax.ppermute(x, axis, [(i, i ^ 1 << apart) for i in range(lax.axis_size(axis))])


def complex_dot(left_mat, right_mat, precision=precise):
    def dot(x, y):
        return jnp.dot(x, y, precision=precision, preferred_element_type=jnp.float32)

    real_part = dot(left_mat[0], right_mat[0]) - dot(left_mat[1], right_mat[1])
    imag_part = dot(left_mat[0], right_mat[1]) + dot(left_mat[1], right_mat[0])
    return jnp.stack([real_part, imag_part])


def side_dot(vectors, matrix, precision=precise):
    return lax.dot_general(
        vectors,
        matrix,
        (((1,), (1,)), ((), ())),
        precision=precision,
        preferred_element_type=jnp.float32,
    )


def complex_apply(matrix, vectors, precision=precise):
    real_part = side_dot(vectors[0], matrix[0], precision) - side_dot(vectors[1], matrix[1], precision)
    imag_part = side_dot(vectors[0], matrix[1], precision) + side_dot(vectors[1], matrix[0], precision)
    return jnp.stack([real_part, imag_part])


def complex_solve(system, right_mat):
    size_n = system.shape[1]
    upper_band = jnp.concatenate([system[0], -system[1]], 1)
    lower_band = jnp.concatenate([system[1], system[0]], 1)
    big_mat = jnp.concatenate([upper_band, lower_band], 0)
    stacked = jnp.concatenate([right_mat[0], right_mat[1]], 0)
    normal = lax.dot_general(
        big_mat,
        big_mat,
        (((0,), (0,)), ((), ())),
        precision=precise,
        preferred_element_type=jnp.float32,
    )
    projected = lax.dot_general(
        big_mat,
        stacked,
        (((0,), (0,)), ((), ())),
        precision=precise,
        preferred_element_type=jnp.float32,
    )
    factor = jnp.linalg.cholesky(normal)
    solution = jax.scipy.linalg.cho_solve((factor, True), projected)
    return jnp.stack([solution[:size_n], solution[size_n:]])


def block_take(matrix, row_list, col_list):
    row_cat = jnp.concatenate([matrix[:, start_at:stop_at] for start_at, stop_at in row_list], 1)
    return jnp.concatenate([row_cat[:, :, start_at:stop_at] for start_at, stop_at in col_list], 2)


def rows_lower(blocks, solved):
    alpha_outer, alpha_reach = (blocks[0], blocks[1])
    upper_count = solved.shape[2] - alpha_outer.shape[2]
    padded = jnp.concatenate(
        [alpha_outer, jnp.zeros((2, alpha_outer.shape[1], upper_count), jnp.float32)], 2
    )
    return padded - complex_dot(alpha_reach, solved)


def rows_upper(blocks, solved):
    alpha_inward, alpha_inner, beta_outer, beta_reach = (blocks[2], blocks[3], blocks[4], blocks[5])
    leading = jnp.concatenate([-complex_dot(beta_reach, alpha_inward), beta_outer], 2)
    return leading + complex_dot(complex_dot(beta_reach, alpha_inner), solved)


def order_spans(side_pts, edge_pts, keeping):
    lower_ext = 2 * side_pts + (edge_pts if keeping else 0)
    starts = [
        (0, side_pts),
        (lower_ext, side_pts),
        (side_pts, side_pts),
        (lower_ext + side_pts, side_pts),
    ]
    if keeping:
        starts = starts + [(2 * side_pts, edge_pts), (lower_ext + 2 * side_pts, edge_pts)]
    return [(start_at, start_at + length) for start_at, length in starts]


def incident(position, thetas, face_pts, edge_pts):
    heights = (jnp.arange(face_pts, dtype=jnp.float32) + 0.5) / edge_pts
    across_x = jnp.cos(thetas)[:, None]
    along_y = jnp.sin(thetas)[:, None]
    left_phase = wavenumber * (position * across_x + heights[None, :] * along_y)
    right_phase = wavenumber * ((position + 1.0) * across_x + heights[None, :] * along_y)
    phases = jnp.concatenate([left_phase, right_phase], 1)
    return jnp.stack([jnp.cos(phases), jnp.sin(phases)])


def shifted_along(x, axis, pairs):
    return lax.ppermute(x, axis, pairs)


def role_spans(side_pts, edge_pts, keeping, lower):
    total_pts = 2 * side_pts + 2 * edge_pts
    if lower:
        outer = [(0, 2 * side_pts + (edge_pts if keeping else 0))]
        inner = [(2 * side_pts + edge_pts, total_pts)]
    else:
        outer = [(0, 2 * side_pts)] + ([(2 * side_pts + edge_pts, total_pts)] if keeping else [])
        inner = [(2 * side_pts, 2 * side_pts + edge_pts)]
    return outer, inner


def split_map(matrix, side_pts, edge_pts, keeping, lower):
    outer, inner = role_spans(side_pts, edge_pts, keeping, lower)
    cols = outer + inner
    return block_take(matrix, inner, cols), block_take(matrix, outer, cols)


def merge_parts(lower_in, lower_out, upper_in, upper_out, side_pts, edge_pts, keeping):
    n_ao = lower_out.shape[1]
    n_bo = upper_out.shape[1]
    alpha_outer = lower_out[:, :, :n_ao]
    alpha_reach = lower_out[:, :, n_ao:]
    alpha_inward = lower_in[:, :, :n_ao]
    alpha_inner = lower_in[:, :, n_ao:]
    beta_outer = upper_out[:, :, :n_bo]
    beta_reach = upper_out[:, :, n_bo:]
    beta_inward = upper_in[:, :, :n_bo]
    beta_inner = upper_in[:, :, n_bo:]
    identity_mat = jnp.stack(
        [jnp.eye(edge_pts, dtype=jnp.float32), jnp.zeros((edge_pts, edge_pts), jnp.float32)]
    )
    system = identity_mat - complex_dot(beta_inner, alpha_inner)
    right_mat = jnp.concatenate([-complex_dot(beta_inner, alpha_inward), beta_inward], 2)
    solved = complex_solve(system, right_mat)
    blocks = (alpha_outer, alpha_reach, alpha_inward, alpha_inner, beta_outer, beta_reach)
    merged = jnp.concatenate([rows_lower(blocks, solved), rows_upper(blocks, solved)], 1)
    span_list = order_spans(side_pts, edge_pts, keeping)
    return block_take(merged, span_list, span_list)


def exchange_merge(own, spare, own_is_lower, axis, apart, side_pts, edge_pts, keeping):
    spare_lo = split_map(spare, side_pts, edge_pts, keeping, True)
    spare_up = split_map(spare, side_pts, edge_pts, keeping, False)
    send_in = jnp.where(own_is_lower, spare_lo[0], spare_up[0])
    send_out = jnp.where(own_is_lower, spare_lo[1], spare_up[1])
    got_in = from_partner(send_in, axis, apart)
    got_in, send_out = lax.optimization_barrier((got_in, send_out))
    got_out = from_partner(send_out, axis, apart)
    own_lo = split_map(own, side_pts, edge_pts, keeping, True)
    own_up = split_map(own, side_pts, edge_pts, keeping, False)
    lower_in = jnp.where(own_is_lower, own_lo[0], got_in)
    lower_out = jnp.where(own_is_lower, own_lo[1], got_out)
    upper_in = jnp.where(own_is_lower, got_in, own_up[0])
    upper_out = jnp.where(own_is_lower, got_out, own_up[1])
    return merge_parts(lower_in, lower_out, upper_in, upper_out, side_pts, edge_pts, keeping)


def real_block(matrix):
    return jnp.concatenate(
        [
            jnp.concatenate([matrix[0].T, matrix[1].T], 1),
            jnp.concatenate([-matrix[1].T, matrix[0].T], 1),
        ],
        0,
    )


def per_device_body(leaf_maps, angles):
    edge_pts = leaf_maps.shape[-1] // 4
    leaf_id = lax.axis_index("leaf")
    pol_id = leaf_id % 2
    half_id = leaf_id // 2
    own_maps = leaf_maps[0, 0]
    own_pol = lax.dynamic_index_in_dim(own_maps, pol_id, 0, keepdims=False)
    other_pol = lax.dynamic_index_in_dim(own_maps, 1 - pol_id, 0, keepdims=False)
    paired = exchange_merge(own_pol, other_pol, pol_id == 0, "leaf", 0, edge_pts, edge_pts, True)
    full_map = exchange_merge(paired, paired, half_id == 0, "leaf", 1, 2 * edge_pts, edge_pts, False)
    face_pts = full_map.shape[1] // 2
    col_count = angles.shape[0] // 2
    thetas = lax.dynamic_slice_in_dim(angles, half_id * col_count, col_count)
    wide_id = lax.axis_index("wide")
    wide_count = lax.axis_size("wide")
    position = wide_id.astype(jnp.float32)
    incoming = incident(position, thetas, face_pts, edge_pts)
    driven = complex_apply(full_map, incoming)
    transfer = full_map[:, face_pts:, :face_pts]
    outgoing = driven[:, :, face_pts:]

    to_odd = [(i, i + 1) for i in range(0, wide_count, 2)]
    handed = shifted_along(jnp.concatenate([transfer, outgoing], 1), "wide", to_odd)
    prev_transfer = handed[:, :face_pts]
    prev_outgoing = handed[:, face_pts:]
    double_map = complex_dot(transfer, prev_transfer, quick)
    double_drive = outgoing + complex_apply(transfer, prev_outgoing, quick)
    to_quad = [(i, i + 2) for i in range(1, wide_count, 4)]
    handed2 = shifted_along(jnp.concatenate([double_map, double_drive], 1), "wide", to_quad)
    prev_double_map = handed2[:, :face_pts]
    prev_double_drive = handed2[:, face_pts:]
    quad_map = real_block(complex_dot(double_map, prev_double_map, quick))
    quad_drive = double_drive + complex_apply(double_map, prev_double_drive, quick)
    flat_drive = jnp.concatenate([quad_drive[0], quad_drive[1]], 1)
    blank = jnp.zeros_like(flat_drive)

    quad_pairs = [(i, i + 4) for i in range(3, wide_count - 4, 4)]

    def advance(step_at, stored):
        active = wide_id == 4 * step_at + 3
        sending = lax.cond(
            active,
            lambda: flat_drive
            + jnp.dot(stored, quad_map, precision=quick, preferred_element_type=jnp.float32),
            lambda: blank,
        )
        received = shifted_along(sending, "wide", quad_pairs)
        return jnp.where(wide_id == 4 * step_at + 7, received, stored)

    flat_in = lax.fori_loop(0, wide_count // 4 - 1, advance, blank)
    quad_in = jnp.stack([flat_in[:, :face_pts], flat_in[:, face_pts:]])
    back_pairs = [(i + 2, i) for i in range(1, wide_count, 4)]
    given2 = shifted_along(quad_in, "wide", back_pairs)
    own_next = prev_double_drive + complex_apply(prev_double_map, quad_in, quick)
    even_in = jnp.where(wide_id % 4 == 3, own_next, given2)
    to_even = [(i + 1, i) for i in range(0, wide_count, 2)]
    given = shifted_along(even_in, "wide", to_even)
    is_odd = wide_id % 2 == 1
    odd_in = prev_outgoing + complex_apply(prev_transfer, even_in, quick)
    chained = jnp.where(is_odd, odd_in, given)
    right_part = outgoing + complex_apply(transfer, chained, quick)
    left_part = driven[:, :, :face_pts] + complex_apply(full_map[:, :face_pts, :face_pts], chained, quick)
    return (left_part[None], right_part[None])


def solution(mesh):
    placed = (P("wide", "leaf", None, None, None, None), P())
    return jax.shard_map(
        per_device_body,
        mesh=mesh,
        in_specs=placed,
        out_specs=(P("wide", None, "leaf", None), P("wide", None, "leaf", None)),
        check_vma=False,
    )
```

```python
import jax
import jax.numpy as jnp
from jax import lax
from jax.sharding import PartitionSpec as P

precise = lax.Precision.HIGHEST
quick = lax.Precision.HIGH
wavenumber = 12.0


def from_partner(x, axis, apart):
    return lax.ppermute(x, axis, [(i, i ^ 1 << apart) for i in range(lax.axis_size(axis))])


def complex_dot(left_mat, right_mat, precision=precise):
    def dot(x, y):
        return jnp.dot(x, y, precision=precision, preferred_element_type=jnp.float32)

    real_part = dot(left_mat[0], right_mat[0]) - dot(left_mat[1], right_mat[1])
    imag_part = dot(left_mat[0], right_mat[1]) + dot(left_mat[1], right_mat[0])
    return jnp.stack([real_part, imag_part])


def side_dot(vectors, matrix, precision=precise):
    return lax.dot_general(
        vectors,
        matrix,
        (((1,), (1,)), ((), ())),
        precision=precision,
        preferred_element_type=jnp.float32,
    )


def complex_apply(matrix, vectors, precision=precise):
    real_part = side_dot(vectors[0], matrix[0], precision) - side_dot(vectors[1], matrix[1], precision)
    imag_part = side_dot(vectors[0], matrix[1], precision) + side_dot(vectors[1], matrix[0], precision)
    return jnp.stack([real_part, imag_part])


def complex_solve(system, right_mat):
    size_n = system.shape[1]
    upper_band = jnp.concatenate([system[0], -system[1]], 1)
    lower_band = jnp.concatenate([system[1], system[0]], 1)
    big_mat = jnp.concatenate([upper_band, lower_band], 0)
    stacked = jnp.concatenate([right_mat[0], right_mat[1]], 0)
    normal = lax.dot_general(
        big_mat,
        big_mat,
        (((0,), (0,)), ((), ())),
        precision=precise,
        preferred_element_type=jnp.float32,
    )
    projected = lax.dot_general(
        big_mat,
        stacked,
        (((0,), (0,)), ((), ())),
        precision=precise,
        preferred_element_type=jnp.float32,
    )
    factor = jnp.linalg.cholesky(normal)
    solution = jax.scipy.linalg.cho_solve((factor, True), projected)
    return jnp.stack([solution[:size_n], solution[size_n:]])


def block_take(matrix, row_list, col_list):
    row_cat = jnp.concatenate([matrix[:, start_at:stop_at] for start_at, stop_at in row_list], 1)
    return jnp.concatenate([row_cat[:, :, start_at:stop_at] for start_at, stop_at in col_list], 2)


def rows_lower(blocks, solved, precision=precise):
    alpha_outer, alpha_reach = (blocks[0], blocks[1])
    upper_count = solved.shape[2] - alpha_outer.shape[2]
    padded = jnp.concatenate(
        [alpha_outer, jnp.zeros((2, alpha_outer.shape[1], upper_count), jnp.float32)], 2
    )
    return padded - complex_dot(alpha_reach, solved, precision)


def rows_upper(blocks, solved, precision=precise):
    alpha_inward, alpha_inner, beta_outer, beta_reach = (blocks[2], blocks[3], blocks[4], blocks[5])
    leading = jnp.concatenate([-complex_dot(beta_reach, alpha_inward, precision), beta_outer], 2)
    return leading + complex_dot(complex_dot(beta_reach, alpha_inner, precision), solved, precision)


def order_spans(side_pts, edge_pts, keeping):
    lower_ext = 2 * side_pts + (edge_pts if keeping else 0)
    starts = [
        (0, side_pts),
        (lower_ext, side_pts),
        (side_pts, side_pts),
        (lower_ext + side_pts, side_pts),
    ]
    if keeping:
        starts = starts + [(2 * side_pts, edge_pts), (lower_ext + 2 * side_pts, edge_pts)]
    return [(start_at, start_at + length) for start_at, length in starts]


def incident(position, thetas, face_pts, edge_pts):
    heights = (jnp.arange(face_pts, dtype=jnp.float32) + 0.5) / edge_pts
    across_x = jnp.cos(thetas)[:, None]
    along_y = jnp.sin(thetas)[:, None]
    left_phase = wavenumber * (position * across_x + heights[None, :] * along_y)
    right_phase = wavenumber * ((position + 1.0) * across_x + heights[None, :] * along_y)
    phases = jnp.concatenate([left_phase, right_phase], 1)
    return jnp.stack([jnp.cos(phases), jnp.sin(phases)])


def shifted_along(x, axis, pairs):
    return lax.ppermute(x, axis, pairs)


def role_spans(side_pts, edge_pts, keeping, lower):
    total_pts = 2 * side_pts + 2 * edge_pts
    if lower:
        outer = [(0, 2 * side_pts + (edge_pts if keeping else 0))]
        inner = [(2 * side_pts + edge_pts, total_pts)]
    else:
        outer = [(0, 2 * side_pts)] + ([(2 * side_pts + edge_pts, total_pts)] if keeping else [])
        inner = [(2 * side_pts, 2 * side_pts + edge_pts)]
    return outer, inner


def split_map(matrix, side_pts, edge_pts, keeping, lower):
    outer, inner = role_spans(side_pts, edge_pts, keeping, lower)
    cols = outer + inner
    return block_take(matrix, inner, cols), block_take(matrix, outer, cols)


def merge_parts(lower_in, lower_out, upper_in, upper_out, side_pts, edge_pts, keeping):
    n_ao = lower_out.shape[1]
    n_bo = upper_out.shape[1]
    alpha_outer = lower_out[:, :, :n_ao]
    alpha_reach = lower_out[:, :, n_ao:]
    alpha_inward = lower_in[:, :, :n_ao]
    alpha_inner = lower_in[:, :, n_ao:]
    beta_outer = upper_out[:, :, :n_bo]
    beta_reach = upper_out[:, :, n_bo:]
    beta_inward = upper_in[:, :, :n_bo]
    beta_inner = upper_in[:, :, n_bo:]
    identity_mat = jnp.stack(
        [jnp.eye(edge_pts, dtype=jnp.float32), jnp.zeros((edge_pts, edge_pts), jnp.float32)]
    )
    system = identity_mat - complex_dot(beta_inner, alpha_inner)
    right_mat = jnp.concatenate([-complex_dot(beta_inner, alpha_inward), beta_inward], 2)
    solved = complex_solve(system, right_mat)
    blocks = (alpha_outer, alpha_reach, alpha_inward, alpha_inner, beta_outer, beta_reach)
    row_precision = precise if keeping else quick
    merged = jnp.concatenate(
        [rows_lower(blocks, solved, row_precision), rows_upper(blocks, solved, row_precision)], 1
    )
    span_list = order_spans(side_pts, edge_pts, keeping)
    return block_take(merged, span_list, span_list)


def exchange_merge(own, spare, own_is_lower, axis, apart, side_pts, edge_pts, keeping):
    spare_lo = split_map(spare, side_pts, edge_pts, keeping, True)
    spare_up = split_map(spare, side_pts, edge_pts, keeping, False)
    send_in = jnp.where(own_is_lower, spare_lo[0], spare_up[0])
    send_out = jnp.where(own_is_lower, spare_lo[1], spare_up[1])
    got_in = from_partner(send_in, axis, apart)
    got_in, send_out = lax.optimization_barrier((got_in, send_out))
    got_out = from_partner(send_out, axis, apart)
    own_lo = split_map(own, side_pts, edge_pts, keeping, True)
    own_up = split_map(own, side_pts, edge_pts, keeping, False)
    lower_in = jnp.where(own_is_lower, own_lo[0], got_in)
    lower_out = jnp.where(own_is_lower, own_lo[1], got_out)
    upper_in = jnp.where(own_is_lower, got_in, own_up[0])
    upper_out = jnp.where(own_is_lower, got_out, own_up[1])
    return merge_parts(lower_in, lower_out, upper_in, upper_out, side_pts, edge_pts, keeping)


def real_block(matrix):
    return jnp.concatenate(
        [
            jnp.concatenate([matrix[0].T, matrix[1].T], 1),
            jnp.concatenate([-matrix[1].T, matrix[0].T], 1),
        ],
        0,
    )


def per_device_body(leaf_maps, angles):
    edge_pts = leaf_maps.shape[-1] // 4
    leaf_id = lax.axis_index("leaf")
    pol_id = leaf_id % 2
    half_id = leaf_id // 2
    own_maps = leaf_maps[0, 0]
    own_pol = lax.dynamic_index_in_dim(own_maps, pol_id, 0, keepdims=False)
    other_pol = lax.dynamic_index_in_dim(own_maps, 1 - pol_id, 0, keepdims=False)
    paired = exchange_merge(own_pol, other_pol, pol_id == 0, "leaf", 0, edge_pts, edge_pts, True)
    full_map = exchange_merge(paired, paired, half_id == 0, "leaf", 1, 2 * edge_pts, edge_pts, False)
    face_pts = full_map.shape[1] // 2
    col_count = angles.shape[0] // 2
    thetas = lax.dynamic_slice_in_dim(angles, half_id * col_count, col_count)
    wide_id = lax.axis_index("wide")
    wide_count = lax.axis_size("wide")
    position = wide_id.astype(jnp.float32)
    incoming = incident(position, thetas, face_pts, edge_pts)
    driven = complex_apply(full_map, incoming, quick)
    transfer = full_map[:, face_pts:, :face_pts]
    outgoing = driven[:, :, face_pts:]

    to_odd = [(i, i + 1) for i in range(0, wide_count, 2)]
    handed = shifted_along(jnp.concatenate([transfer, outgoing], 1), "wide", to_odd)
    prev_transfer = handed[:, :face_pts]
    prev_outgoing = handed[:, face_pts:]
    double_map = complex_dot(transfer, prev_transfer, quick)
    double_drive = outgoing + complex_apply(transfer, prev_outgoing, quick)
    to_quad = [(i, i + 2) for i in range(1, wide_count, 4)]
    handed2 = shifted_along(jnp.concatenate([double_map, double_drive], 1), "wide", to_quad)
    prev_double_map = handed2[:, :face_pts]
    prev_double_drive = handed2[:, face_pts:]
    quad_map = real_block(complex_dot(double_map, prev_double_map, quick))
    quad_drive = double_drive + complex_apply(double_map, prev_double_drive, quick)
    flat_drive = jnp.concatenate([quad_drive[0], quad_drive[1]], 1)
    blank = jnp.zeros_like(flat_drive)

    quad_pairs = [(i, i + 4) for i in range(3, wide_count - 4, 4)]

    def advance(step_at, stored):
        active = wide_id == 4 * step_at + 3
        sending = lax.cond(
            active,
            lambda: flat_drive
            + jnp.dot(stored, quad_map, precision=quick, preferred_element_type=jnp.float32),
            lambda: blank,
        )
        received = shifted_along(sending, "wide", quad_pairs)
        return jnp.where(wide_id == 4 * step_at + 7, received, stored)

    flat_in = lax.fori_loop(0, wide_count // 4 - 1, advance, blank)
    quad_in = jnp.stack([flat_in[:, :face_pts], flat_in[:, face_pts:]])
    back_pairs = [(i + 2, i) for i in range(1, wide_count, 4)]
    given2 = shifted_along(quad_in, "wide", back_pairs)
    own_next = prev_double_drive + complex_apply(prev_double_map, quad_in, quick)
    even_in = jnp.where(wide_id % 4 == 3, own_next, given2)
    to_even = [(i + 1, i) for i in range(0, wide_count, 2)]
    given = shifted_along(even_in, "wide", to_even)
    is_odd = wide_id % 2 == 1
    odd_in = prev_outgoing + complex_apply(prev_transfer, even_in, quick)
    chained = jnp.where(is_odd, odd_in, given)
    right_part = outgoing + complex_apply(transfer, chained, quick)
    left_part = driven[:, :, :face_pts] + complex_apply(full_map[:, :face_pts, :face_pts], chained, quick)
    return (left_part[None], right_part[None])


def solution(mesh):
    placed = (P("wide", "leaf", None, None, None, None), P())
    return jax.shard_map(
        per_device_body,
        mesh=mesh,
        in_specs=placed,
        out_specs=(P("wide", None, "leaf", None), P("wide", None, "leaf", None)),
        check_vma=False,
    )
```

```python
import jax
import jax.numpy as jnp
from jax import lax
from jax.sharding import PartitionSpec as P

precise = lax.Precision.HIGHEST
quick = lax.Precision.HIGH
wavenumber = 12.0


def from_partner(x, axis, apart):
    return lax.ppermute(x, axis, [(i, i ^ 1 << apart) for i in range(lax.axis_size(axis))])


def complex_dot(left_mat, right_mat, precision=precise):
    def dot(x, y):
        return jnp.dot(x, y, precision=precision, preferred_element_type=jnp.float32)

    real_part = dot(left_mat[0], right_mat[0]) - dot(left_mat[1], right_mat[1])
    imag_part = dot(left_mat[0], right_mat[1]) + dot(left_mat[1], right_mat[0])
    return jnp.stack([real_part, imag_part])


def side_dot(vectors, matrix, precision=precise):
    return lax.dot_general(
        vectors,
        matrix,
        (((1,), (1,)), ((), ())),
        precision=precision,
        preferred_element_type=jnp.float32,
    )


def complex_apply(matrix, vectors, precision=precise):
    real_part = side_dot(vectors[0], matrix[0], precision) - side_dot(vectors[1], matrix[1], precision)
    imag_part = side_dot(vectors[0], matrix[1], precision) + side_dot(vectors[1], matrix[0], precision)
    return jnp.stack([real_part, imag_part])


def complex_solve(system, right_mat):
    size_n = system.shape[1]
    upper_band = jnp.concatenate([system[0], -system[1]], 1)
    lower_band = jnp.concatenate([system[1], system[0]], 1)
    big_mat = jnp.concatenate([upper_band, lower_band], 0)
    stacked = jnp.concatenate([right_mat[0], right_mat[1]], 0)
    normal = lax.dot_general(
        big_mat,
        big_mat,
        (((0,), (0,)), ((), ())),
        precision=precise,
        preferred_element_type=jnp.float32,
    )
    projected = lax.dot_general(
        big_mat,
        stacked,
        (((0,), (0,)), ((), ())),
        precision=precise,
        preferred_element_type=jnp.float32,
    )
    factor = jnp.linalg.cholesky(normal)
    solution = jax.scipy.linalg.cho_solve((factor, True), projected)
    return jnp.stack([solution[:size_n], solution[size_n:]])


def block_take(matrix, row_list, col_list):
    row_cat = jnp.concatenate([matrix[:, start_at:stop_at] for start_at, stop_at in row_list], 1)
    return jnp.concatenate([row_cat[:, :, start_at:stop_at] for start_at, stop_at in col_list], 2)


def rows_lower(blocks, solved, precision=precise):
    alpha_outer, alpha_reach = (blocks[0], blocks[1])
    upper_count = solved.shape[2] - alpha_outer.shape[2]
    padded = jnp.concatenate(
        [alpha_outer, jnp.zeros((2, alpha_outer.shape[1], upper_count), jnp.float32)], 2
    )
    return padded - complex_dot(alpha_reach, solved, precision)


def rows_upper(blocks, solved, precision=precise):
    alpha_inward, alpha_inner, beta_outer, beta_reach = (blocks[2], blocks[3], blocks[4], blocks[5])
    leading = jnp.concatenate([-complex_dot(beta_reach, alpha_inward, precision), beta_outer], 2)
    return leading + complex_dot(complex_dot(beta_reach, alpha_inner, precision), solved, precision)


def order_spans(side_pts, edge_pts, keeping):
    lower_ext = 2 * side_pts + (edge_pts if keeping else 0)
    starts = [
        (0, side_pts),
        (lower_ext, side_pts),
        (side_pts, side_pts),
        (lower_ext + side_pts, side_pts),
    ]
    if keeping:
        starts = starts + [(2 * side_pts, edge_pts), (lower_ext + 2 * side_pts, edge_pts)]
    return [(start_at, start_at + length) for start_at, length in starts]


def incident(position, thetas, face_pts, edge_pts):
    heights = (jnp.arange(face_pts, dtype=jnp.float32) + 0.5) / edge_pts
    across_x = jnp.cos(thetas)[:, None]
    along_y = jnp.sin(thetas)[:, None]
    left_phase = wavenumber * (position * across_x + heights[None, :] * along_y)
    right_phase = wavenumber * ((position + 1.0) * across_x + heights[None, :] * along_y)
    phases = jnp.concatenate([left_phase, right_phase], 1)
    return jnp.stack([jnp.cos(phases), jnp.sin(phases)])


def shifted_along(x, axis, pairs):
    return lax.ppermute(x, axis, pairs)


def role_spans(side_pts, edge_pts, keeping, lower):
    total_pts = 2 * side_pts + 2 * edge_pts
    if lower:
        outer = [(0, 2 * side_pts + (edge_pts if keeping else 0))]
        inner = [(2 * side_pts + edge_pts, total_pts)]
    else:
        outer = [(0, 2 * side_pts)] + ([(2 * side_pts + edge_pts, total_pts)] if keeping else [])
        inner = [(2 * side_pts, 2 * side_pts + edge_pts)]
    return outer, inner


def split_map(matrix, side_pts, edge_pts, keeping, lower):
    outer, inner = role_spans(side_pts, edge_pts, keeping, lower)
    cols = outer + inner
    return block_take(matrix, inner, cols), block_take(matrix, outer, cols)


def merge_parts(lower_in, lower_out, upper_in, upper_out, side_pts, edge_pts, keeping):
    n_ao = lower_out.shape[1]
    n_bo = upper_out.shape[1]
    alpha_outer = lower_out[:, :, :n_ao]
    alpha_reach = lower_out[:, :, n_ao:]
    alpha_inward = lower_in[:, :, :n_ao]
    alpha_inner = lower_in[:, :, n_ao:]
    beta_outer = upper_out[:, :, :n_bo]
    beta_reach = upper_out[:, :, n_bo:]
    beta_inward = upper_in[:, :, :n_bo]
    beta_inner = upper_in[:, :, n_bo:]
    identity_mat = jnp.stack(
        [jnp.eye(edge_pts, dtype=jnp.float32), jnp.zeros((edge_pts, edge_pts), jnp.float32)]
    )
    system = identity_mat - complex_dot(beta_inner, alpha_inner)
    right_mat = jnp.concatenate([-complex_dot(beta_inner, alpha_inward), beta_inward], 2)
    solved = complex_solve(system, right_mat)
    blocks = (alpha_outer, alpha_reach, alpha_inward, alpha_inner, beta_outer, beta_reach)
    row_precision = precise if keeping else quick
    merged = jnp.concatenate(
        [rows_lower(blocks, solved, row_precision), rows_upper(blocks, solved, row_precision)], 1
    )
    span_list = order_spans(side_pts, edge_pts, keeping)
    return block_take(merged, span_list, span_list)


def exchange_merge(own, spare, own_is_lower, axis, apart, side_pts, edge_pts, keeping):
    spare_lo = split_map(spare, side_pts, edge_pts, keeping, True)
    spare_up = split_map(spare, side_pts, edge_pts, keeping, False)
    send_in = jnp.where(own_is_lower, spare_lo[0], spare_up[0])
    send_out = jnp.where(own_is_lower, spare_lo[1], spare_up[1])
    got_in = from_partner(send_in, axis, apart)
    got_in, send_out = lax.optimization_barrier((got_in, send_out))
    got_out = from_partner(send_out, axis, apart)
    own_lo = split_map(own, side_pts, edge_pts, keeping, True)
    own_up = split_map(own, side_pts, edge_pts, keeping, False)
    lower_in = jnp.where(own_is_lower, own_lo[0], got_in)
    lower_out = jnp.where(own_is_lower, own_lo[1], got_out)
    upper_in = jnp.where(own_is_lower, got_in, own_up[0])
    upper_out = jnp.where(own_is_lower, got_out, own_up[1])
    return merge_parts(lower_in, lower_out, upper_in, upper_out, side_pts, edge_pts, keeping)


def real_block(matrix):
    return jnp.concatenate(
        [
            jnp.concatenate([matrix[0].T, matrix[1].T], 1),
            jnp.concatenate([-matrix[1].T, matrix[0].T], 1),
        ],
        0,
    )


def per_device_body(leaf_maps, angles):
    edge_pts = leaf_maps.shape[-1] // 4
    leaf_id = lax.axis_index("leaf")
    pol_id = leaf_id % 2
    half_id = leaf_id // 2
    own_maps = leaf_maps[0, 0]
    own_pol = lax.dynamic_index_in_dim(own_maps, pol_id, 0, keepdims=False)
    other_pol = lax.dynamic_index_in_dim(own_maps, 1 - pol_id, 0, keepdims=False)
    paired = exchange_merge(own_pol, other_pol, pol_id == 0, "leaf", 0, edge_pts, edge_pts, True)
    full_map = exchange_merge(paired, paired, half_id == 0, "leaf", 1, 2 * edge_pts, edge_pts, False)
    face_pts = full_map.shape[1] // 2
    col_count = angles.shape[0] // 2
    thetas = lax.dynamic_slice_in_dim(angles, half_id * col_count, col_count)
    wide_id = lax.axis_index("wide")
    wide_count = lax.axis_size("wide")
    position = wide_id.astype(jnp.float32)
    incoming = incident(position, thetas, face_pts, edge_pts)
    driven = complex_apply(full_map, incoming, quick)
    transfer = full_map[:, face_pts:, :face_pts]
    outgoing = driven[:, :, face_pts:]

    to_odd = [(i, i + 1) for i in range(0, wide_count, 2)]
    handed = shifted_along(jnp.concatenate([transfer, outgoing], 1), "wide", to_odd)
    prev_transfer = handed[:, :face_pts]
    prev_outgoing = handed[:, face_pts:]
    double_map = complex_dot(transfer, prev_transfer, quick)
    double_drive = outgoing + complex_apply(transfer, prev_outgoing, quick)
    to_quad = [(i, i + 2) for i in range(1, wide_count, 4)]
    handed2 = shifted_along(jnp.concatenate([double_map, double_drive], 1), "wide", to_quad)
    prev_double_map = handed2[:, :face_pts]
    prev_double_drive = handed2[:, face_pts:]
    quad_map = real_block(complex_dot(double_map, prev_double_map, quick))
    quad_drive = double_drive + complex_apply(double_map, prev_double_drive, quick)
    flat_drive = jnp.concatenate([quad_drive[0], quad_drive[1]], 1)
    blank = jnp.zeros_like(flat_drive)

    quad_pairs = [(i, i + 4) for i in range(3, wide_count - 4, 4)]

    def advance(step_at, stored):
        active = wide_id == 4 * step_at + 3
        sending = lax.cond(
            active,
            lambda: flat_drive
            + jnp.dot(stored, quad_map, precision=quick, preferred_element_type=jnp.float32),
            lambda: blank,
        )
        received = shifted_along(sending, "wide", quad_pairs)
        return jnp.where(wide_id == 4 * step_at + 7, received, stored)

    flat_in = lax.fori_loop(0, wide_count // 4 - 1, advance, blank)
    quad_in = jnp.stack([flat_in[:, :face_pts], flat_in[:, face_pts:]])
    to_second = [(i + 2, i) for i in range(1, wide_count, 4)]
    to_first = [(i + 3, i) for i in range(0, wide_count, 4)]
    to_third = [(i + 1, i) for i in range(2, wide_count, 4)]
    given_second = shifted_along(quad_in, "wide", to_second)
    given_first = shifted_along(quad_in, "wide", to_first)
    own_next = prev_double_drive + complex_apply(prev_double_map, quad_in, quick)
    given_third = shifted_along(own_next, "wide", to_third)
    place = wide_id % 4
    even_in = jnp.where(place == 3, own_next, given_second)
    odd_in = prev_outgoing + complex_apply(prev_transfer, even_in, quick)
    chained = jnp.where(place % 2 == 1, odd_in, jnp.where(place == 0, given_first, given_third))
    right_part = outgoing + complex_apply(transfer, chained, quick)
    left_part = driven[:, :, :face_pts] + complex_apply(full_map[:, :face_pts, :face_pts], chained, quick)
    return (left_part[None], right_part[None])


def solution(mesh):
    placed = (P("wide", "leaf", None, None, None, None), P())
    return jax.shard_map(
        per_device_body,
        mesh=mesh,
        in_specs=placed,
        out_specs=(P("wide", None, "leaf", None), P("wide", None, "leaf", None)),
        check_vma=False,
    )
```

```python
import jax
import jax.numpy as jnp
from jax import lax
from jax.sharding import PartitionSpec as P

precise = lax.Precision.HIGHEST
quick = lax.Precision.HIGH
wavenumber = 12.0


def from_partner(x, axis, apart):
    return lax.ppermute(x, axis, [(i, i ^ 1 << apart) for i in range(lax.axis_size(axis))])


def complex_dot(left_mat, right_mat, precision=precise):
    def dot(x, y):
        return jnp.dot(x, y, precision=precision, preferred_element_type=jnp.float32)

    real_part = dot(left_mat[0], right_mat[0]) - dot(left_mat[1], right_mat[1])
    imag_part = dot(left_mat[0], right_mat[1]) + dot(left_mat[1], right_mat[0])
    return jnp.stack([real_part, imag_part])


def side_dot(vectors, matrix, precision=precise):
    return lax.dot_general(
        vectors,
        matrix,
        (((1,), (1,)), ((), ())),
        precision=precision,
        preferred_element_type=jnp.float32,
    )


def complex_apply(matrix, vectors, precision=precise):
    real_part = side_dot(vectors[0], matrix[0], precision) - side_dot(vectors[1], matrix[1], precision)
    imag_part = side_dot(vectors[0], matrix[1], precision) + side_dot(vectors[1], matrix[0], precision)
    return jnp.stack([real_part, imag_part])


def complex_solve(system, right_mat):
    size_n = system.shape[1]
    upper_band = jnp.concatenate([system[0], -system[1]], 1)
    lower_band = jnp.concatenate([system[1], system[0]], 1)
    big_mat = jnp.concatenate([upper_band, lower_band], 0)
    stacked = jnp.concatenate([right_mat[0], right_mat[1]], 0)
    normal = lax.dot_general(
        big_mat,
        big_mat,
        (((0,), (0,)), ((), ())),
        precision=precise,
        preferred_element_type=jnp.float32,
    )
    projected = lax.dot_general(
        big_mat,
        stacked,
        (((0,), (0,)), ((), ())),
        precision=precise,
        preferred_element_type=jnp.float32,
    )
    factor = jnp.linalg.cholesky(normal)
    solution = jax.scipy.linalg.cho_solve((factor, True), projected)
    return jnp.stack([solution[:size_n], solution[size_n:]])


def block_take(matrix, row_list, col_list):
    row_cat = jnp.concatenate([matrix[:, start_at:stop_at] for start_at, stop_at in row_list], 1)
    return jnp.concatenate([row_cat[:, :, start_at:stop_at] for start_at, stop_at in col_list], 2)


def rows_lower(blocks, solved, precision=precise):
    alpha_outer, alpha_reach = (blocks[0], blocks[1])
    upper_count = solved.shape[2] - alpha_outer.shape[2]
    padded = jnp.concatenate(
        [alpha_outer, jnp.zeros((2, alpha_outer.shape[1], upper_count), jnp.float32)], 2
    )
    return padded - complex_dot(alpha_reach, solved, precision)


def rows_upper(blocks, solved, precision=precise):
    alpha_inward, alpha_inner, beta_outer, beta_reach = (blocks[2], blocks[3], blocks[4], blocks[5])
    leading = jnp.concatenate([-complex_dot(beta_reach, alpha_inward, precision), beta_outer], 2)
    return leading + complex_dot(complex_dot(beta_reach, alpha_inner, precision), solved, precision)


def order_spans(side_pts, edge_pts, keeping):
    lower_ext = 2 * side_pts + (edge_pts if keeping else 0)
    starts = [
        (0, side_pts),
        (lower_ext, side_pts),
        (side_pts, side_pts),
        (lower_ext + side_pts, side_pts),
    ]
    if keeping:
        starts = starts + [(2 * side_pts, edge_pts), (lower_ext + 2 * side_pts, edge_pts)]
    return [(start_at, start_at + length) for start_at, length in starts]


def incident(position, thetas, face_pts, edge_pts):
    heights = (jnp.arange(face_pts, dtype=jnp.float32) + 0.5) / edge_pts
    across_x = jnp.cos(thetas)[:, None]
    along_y = jnp.sin(thetas)[:, None]
    left_phase = wavenumber * (position * across_x + heights[None, :] * along_y)
    right_phase = wavenumber * ((position + 1.0) * across_x + heights[None, :] * along_y)
    phases = jnp.concatenate([left_phase, right_phase], 1)
    return jnp.stack([jnp.cos(phases), jnp.sin(phases)])


def shifted_along(x, axis, pairs):
    return lax.ppermute(x, axis, pairs)


def role_spans(side_pts, edge_pts, keeping, lower):
    total_pts = 2 * side_pts + 2 * edge_pts
    if lower:
        outer = [(0, 2 * side_pts + (edge_pts if keeping else 0))]
        inner = [(2 * side_pts + edge_pts, total_pts)]
    else:
        outer = [(0, 2 * side_pts)] + ([(2 * side_pts + edge_pts, total_pts)] if keeping else [])
        inner = [(2 * side_pts, 2 * side_pts + edge_pts)]
    return outer, inner


def split_map(matrix, side_pts, edge_pts, keeping, lower):
    outer, inner = role_spans(side_pts, edge_pts, keeping, lower)
    cols = outer + inner
    return block_take(matrix, inner, cols), block_take(matrix, outer, cols)


def merge_parts(lower_in, lower_out, upper_in, upper_out, side_pts, edge_pts, keeping):
    n_ao = lower_out.shape[1]
    n_bo = upper_out.shape[1]
    alpha_outer = lower_out[:, :, :n_ao]
    alpha_reach = lower_out[:, :, n_ao:]
    alpha_inward = lower_in[:, :, :n_ao]
    alpha_inner = lower_in[:, :, n_ao:]
    beta_outer = upper_out[:, :, :n_bo]
    beta_reach = upper_out[:, :, n_bo:]
    beta_inward = upper_in[:, :, :n_bo]
    beta_inner = upper_in[:, :, n_bo:]
    identity_mat = jnp.stack(
        [jnp.eye(edge_pts, dtype=jnp.float32), jnp.zeros((edge_pts, edge_pts), jnp.float32)]
    )
    system = identity_mat - complex_dot(beta_inner, alpha_inner)
    right_mat = jnp.concatenate([-complex_dot(beta_inner, alpha_inward), beta_inward], 2)
    solved = complex_solve(system, right_mat)
    blocks = (alpha_outer, alpha_reach, alpha_inward, alpha_inner, beta_outer, beta_reach)
    row_precision = quick
    merged = jnp.concatenate(
        [rows_lower(blocks, solved, row_precision), rows_upper(blocks, solved, row_precision)], 1
    )
    span_list = order_spans(side_pts, edge_pts, keeping)
    return block_take(merged, span_list, span_list)


def exchange_merge(own, spare, own_is_lower, axis, apart, side_pts, edge_pts, keeping):
    spare_lo = split_map(spare, side_pts, edge_pts, keeping, True)
    spare_up = split_map(spare, side_pts, edge_pts, keeping, False)
    send_in = jnp.where(own_is_lower, spare_lo[0], spare_up[0])
    send_out = jnp.where(own_is_lower, spare_lo[1], spare_up[1])
    got_in = from_partner(send_in, axis, apart)
    got_in, send_out = lax.optimization_barrier((got_in, send_out))
    got_out = from_partner(send_out, axis, apart)
    own_lo = split_map(own, side_pts, edge_pts, keeping, True)
    own_up = split_map(own, side_pts, edge_pts, keeping, False)
    lower_in = jnp.where(own_is_lower, own_lo[0], got_in)
    lower_out = jnp.where(own_is_lower, own_lo[1], got_out)
    upper_in = jnp.where(own_is_lower, got_in, own_up[0])
    upper_out = jnp.where(own_is_lower, got_out, own_up[1])
    return merge_parts(lower_in, lower_out, upper_in, upper_out, side_pts, edge_pts, keeping)


def real_block(matrix):
    return jnp.concatenate(
        [
            jnp.concatenate([matrix[0].T, matrix[1].T], 1),
            jnp.concatenate([-matrix[1].T, matrix[0].T], 1),
        ],
        0,
    )


def per_device_body(leaf_maps, angles):
    edge_pts = leaf_maps.shape[-1] // 4
    leaf_id = lax.axis_index("leaf")
    pol_id = leaf_id % 2
    half_id = leaf_id // 2
    own_maps = leaf_maps[0, 0]
    own_pol = lax.dynamic_index_in_dim(own_maps, pol_id, 0, keepdims=False)
    other_pol = lax.dynamic_index_in_dim(own_maps, 1 - pol_id, 0, keepdims=False)
    paired = exchange_merge(own_pol, other_pol, pol_id == 0, "leaf", 0, edge_pts, edge_pts, True)
    full_map = exchange_merge(paired, paired, half_id == 0, "leaf", 1, 2 * edge_pts, edge_pts, False)
    face_pts = full_map.shape[1] // 2
    col_count = angles.shape[0] // 2
    thetas = lax.dynamic_slice_in_dim(angles, half_id * col_count, col_count)
    wide_id = lax.axis_index("wide")
    wide_count = lax.axis_size("wide")
    position = wide_id.astype(jnp.float32)
    incoming = incident(position, thetas, face_pts, edge_pts)
    driven = complex_apply(full_map, incoming, quick)
    transfer = full_map[:, face_pts:, :face_pts]
    outgoing = driven[:, :, face_pts:]

    to_odd = [(i, i + 1) for i in range(0, wide_count, 2)]
    handed = shifted_along(jnp.concatenate([transfer, outgoing], 1), "wide", to_odd)
    prev_transfer = handed[:, :face_pts]
    prev_outgoing = handed[:, face_pts:]
    double_map = complex_dot(transfer, prev_transfer, quick)
    double_drive = outgoing + complex_apply(transfer, prev_outgoing, quick)
    to_quad = [(i, i + 2) for i in range(1, wide_count, 4)]
    handed2 = shifted_along(jnp.concatenate([double_map, double_drive], 1), "wide", to_quad)
    prev_double_map = handed2[:, :face_pts]
    prev_double_drive = handed2[:, face_pts:]
    quad_map = real_block(complex_dot(double_map, prev_double_map, quick))
    quad_drive = double_drive + complex_apply(double_map, prev_double_drive, quick)
    flat_drive = jnp.concatenate([quad_drive[0], quad_drive[1]], 1)
    blank = jnp.zeros_like(flat_drive)

    quad_pairs = [(i, i + 4) for i in range(3, wide_count - 4, 4)]

    def advance(step_at, stored):
        active = wide_id == 4 * step_at + 3
        sending = lax.cond(
            active,
            lambda: flat_drive
            + jnp.dot(stored, quad_map, precision=quick, preferred_element_type=jnp.float32),
            lambda: blank,
        )
        received = shifted_along(sending, "wide", quad_pairs)
        return jnp.where(wide_id == 4 * step_at + 7, received, stored)

    first_sent = shifted_along(jnp.where(wide_id == 3, flat_drive, blank), "wide", quad_pairs)
    first_in = jnp.where(wide_id == 7, first_sent, blank)
    flat_in = lax.fori_loop(1, wide_count // 4 - 1, advance, first_in)
    quad_in = jnp.stack([flat_in[:, :face_pts], flat_in[:, face_pts:]])
    to_second = [(i + 2, i) for i in range(1, wide_count, 4)]
    to_first = [(i + 3, i) for i in range(0, wide_count, 4)]
    to_third = [(i + 1, i) for i in range(2, wide_count, 4)]
    given_second = shifted_along(quad_in, "wide", to_second)
    given_first = shifted_along(quad_in, "wide", to_first)
    own_next = prev_double_drive + complex_apply(prev_double_map, quad_in, quick)
    given_third = shifted_along(own_next, "wide", to_third)
    place = wide_id % 4
    even_in = jnp.where(place == 3, own_next, given_second)
    odd_in = prev_outgoing + complex_apply(prev_transfer, even_in, quick)
    chained = jnp.where(place % 2 == 1, odd_in, jnp.where(place == 0, given_first, given_third))
    right_part = outgoing + complex_apply(transfer, chained, quick)
    left_part = driven[:, :, :face_pts] + complex_apply(full_map[:, :face_pts, :face_pts], chained, quick)
    return (left_part[None], right_part[None])


def solution(mesh):
    placed = (P("wide", "leaf", None, None, None, None), P())
    return jax.shard_map(
        per_device_body,
        mesh=mesh,
        in_specs=placed,
        out_specs=(P("wide", None, "leaf", None), P("wide", None, "leaf", None)),
        check_vma=False,
    )
```
